128 devices in a mesh: gx: 8 (over x, core), gy: 16 (over z, y).
Axes of the slice: x: 4, y: 4, z: 4, core: 2. Of those that a mesh axis runs over, the one named last changes fastest.
Arguments:
- thickness: float32 [8, 1024, 2048], P(None, 'gy', 'gx'), may hold values from 1 to 2
- velocity: float32 [2, 8, 1024, 2048], P(None, None, 'gy', 'gx'), may hold values from -3 to 3
- bottom: float32 [1024, 2048], P('gy', 'gx'), may hold values from -2 to 2
- coriolis: float32 [1024, 2048], P('gy', 'gx'), may hold values from -4 to 4
- reduced: float32 [8], replicated, may hold values from 0.2 to 2
Outputs:
- thickness_new: float32 [8, 1024, 2048], P(None, 'gy', 'gx')
- velocity_new: float32 [2, 8, 1024, 2048], P(None, None, 'gy', 'gx')
The draws below stay inside these ranges and needn't reach their ends.
All inputs are finite; a program needn't handle non-finite values.
Results may differ from the reference program's by a relative error of at most 0.00002.
Values sent between devices are 32-bit elements; how exact they have to be, the bound alone decides.
No kernel may reach another device: no remote copies, remote signals or barrier semaphores. Data moves between devices by JAX's collectives and lax.ppermute only.
A program may use at most 128 MiB of HBM per device.

```python
import math
import jax
import jax.numpy as jnp

LEV = 8
NX = 2048
NY = 1024


def shard_levels(key, dims, shards, smallest, high):
    level, own = 1.0, jax.random.fold_in(key, 6)
    for dim, parts in shards:
        heights = jnp.exp(jax.random.uniform(jax.random.fold_in(own, dim), (parts,), jnp.float32, smallest / len(shards), high / len(shards)))
        level = level * jnp.repeat(heights, dims[dim] // parts).reshape([-1 if axis == dim else 1 for axis in range(len(dims))])
    return level


def bell_draw(stream_key, shape, spread, limit, pieces=(), held_as=jnp.bfloat16):
    factor_of = shard_levels(stream_key, shape, pieces, -0.22, 0.18) if pieces else 1.0
    values = jax.random.normal(stream_key, shape, jnp.float32) * spread * factor_of
    return jnp.minimum(jnp.maximum(values, -limit), limit).astype(held_as)


def setup_inputs(seed: int = 0) -> dict:
    key_of = jax.random.split(jax.random.key(seed), 6)
    thickness = jnp.clip(1.0 + 1.0 * jax.random.uniform(key_of[0], (LEV, NY, NX), jnp.float32) ** shard_levels(key_of[0], (LEV, NY, NX), ((1, 16), (2, 8)), -0.2, 0.2), 1.0, 2.0)
    velocity = bell_draw(key_of[1], (2, LEV, NY, NX), 0.3, 3.0, ((2, 16), (3, 8)), jnp.float32)
    bottom = jnp.clip(jax.random.uniform(key_of[2], (NY, NX), jnp.float32, -2.0, 2.0) * shard_levels(key_of[2], (NY, NX), ((0, 16), (1, 8)), -0.4, 0.0), -2.0, 2.0)
    coriolis = jnp.clip(jax.random.uniform(key_of[3], (NY, NX), jnp.float32, -4.0, 4.0) * shard_levels(key_of[3], (NY, NX), ((0, 16), (1, 8)), -0.4, 0.0), -4.0, 4.0)
    reduced = jnp.clip(jnp.exp(jax.random.uniform(key_of[4], (LEV,), jnp.float32, math.log(0.2), math.log(2.0))), 0.2, 2.0)
    return {"thickness": thickness, "velocity": velocity, "bottom": bottom, "coriolis": coriolis, "reduced": reduced}


gravity = 0.5
time_step = 0.1
half_step = 0.05


def eastward(values):
    return jnp.roll(values, -1, axis=-1)


def westward(values):
    return jnp.roll(values, 1, axis=-1)


def northward(values):
    return jnp.roll(values, -1, axis=-2)


def southward(values):
    return jnp.roll(values, 1, axis=-2)


def tendency(thick, along_x, along_y, bottom, coriolis, reduced):
    flux_x = 0.5 * (thick + eastward(thick)) * along_x
    flux_y = 0.5 * (thick + northward(thick)) * along_y
    vorticity = (eastward(along_y) - along_y) - (northward(along_x) - along_x)
    thick_vertex = 0.25 * (thick + eastward(thick) + northward(thick) + eastward(northward(thick)))
    potential = (vorticity + coriolis) / thick_vertex
    kinetic = 0.25 * (along_x * along_x + westward(along_x) * westward(along_x) + along_y * along_y + southward(along_y) * southward(along_y))
    pressure = gravity * (bottom + jnp.sum(thick, axis=0)) + reduced[:, None, None] * thick
    bernoulli = kinetic + pressure
    rate_thick = -((flux_x - westward(flux_x)) + (flux_y - southward(flux_y)))
    north_flux = potential * (0.5 * (flux_y + eastward(flux_y)))
    rate_x = 0.5 * (southward(north_flux) + north_flux) - (eastward(bernoulli) - bernoulli)
    east_flux = potential * (0.5 * (flux_x + northward(flux_x)))
    rate_y = -0.5 * (westward(east_flux) + east_flux) - (northward(bernoulli) - bernoulli)
    return rate_thick, rate_x, rate_y


def extend(values):
    wrapped = jnp.concatenate([values[..., -1:, :], values, values[..., :1, :]], axis=-2)
    widths = [(0, 0)] * (values.ndim - 1) + [(1, 1)]
    return jnp.pad(wrapped, widths)


def crop(values):
    return values[..., 1:-1, 1:-1]


def reference(thickness, velocity, bottom, coriolis, reduced):
    position = jnp.arange(NX, dtype=jnp.int32)
    wall_x = (position < NX - 1).astype(jnp.float32)
    thick_start = thickness
    east_start = velocity[0] * wall_x
    north_start = velocity[1]
    bottom_edge = extend(bottom)
    coriolis_edge = extend(coriolis)

    def rates(thick, along_x, along_y):
        result = tendency(extend(thick), extend(along_x), extend(along_y), bottom_edge, coriolis_edge, reduced)
        return [crop(item) for item in result]

    first = rates(thick_start, east_start, north_start)
    thick_mid = thick_start + time_step * first[0]
    east_mid = (east_start + time_step * first[1]) * wall_x
    north_mid = north_start + time_step * first[2]
    second = rates(thick_mid, east_mid, north_mid)
    thick_end = thick_start + half_step * (first[0] + second[0])
    east_end = (east_start + half_step * (first[1] + second[1])) * wall_x
    north_end = north_start + half_step * (first[2] + second[2])
    return thick_end, jnp.stack([east_end, north_end])
```

```python
import jax
import jax.numpy as jnp
from jax import lax
from jax.experimental import pallas as pl
from jax.experimental.pallas import tpu as pltpu
from jax.sharding import PartitionSpec as P


gravity = 0.5
time_step = 0.1
half_step = 0.05
PAD = 8
LANES = 128
f32 = jnp.float32
VM = pltpu.VMEM
VSPEC = pl.BlockSpec(memory_space=pltpu.VMEM)
ASPEC = pl.BlockSpec(memory_space=pl.ANY)
SSPEC = pl.BlockSpec(memory_space=pltpu.SMEM)


def lane_iota(shape):
    return lax.broadcasted_iota(jnp.int32, shape, len(shape) - 1)


def pin(values):
    return [pltpu.with_memory_space_constraint(item, pltpu.VMEM) for item in values]


def swap_pairs(count, first, periodic):
    pairs = []
    for low in range(first, count, 2):
        high = low + 1
        if high >= count:
            if not periodic:
                continue
            high -= count
        pairs += [(low, high), (high, low)]
    return pairs


def pack_side(fields, bc, tile, column, rows):
    levels = fields[0].shape[0]
    lane = lane_iota((rows[1], LANES))
    first = jnp.zeros((rows[1], LANES), f32)
    second = jnp.zeros((rows[1], LANES), f32)
    for f, ref in enumerate(fields):
        for l in range(levels):
            spot = 16 * f + l
            moved = pltpu.roll(ref[l, tile, pl.ds(*rows), :], (spot - column) % LANES, 1)
            first = jnp.where(lane == spot, moved, first)
            second = jnp.where(lane == spot + 1, moved, second)
    both = jnp.where((lane & 15) < 8, first, pltpu.roll(second, 7, 1))
    for f in range(2):
        item = bc[f, tile, pl.ds(*rows), :]
        for c in range(2):
            spread = jnp.broadcast_to(item[:, column + c : column + c + 1], item.shape)
            start = 48 + 16 * f + 8 * c
            both = jnp.where((lane >= start) & (lane < start + 8), spread, both)
    return both


def load_kernel(h_hbm, vel_hbm, bot_hbm, cor_hbm, h_ref, u_ref, v_ref, bc_ref, a_ref, b_ref, sem):
    rows = h_hbm.shape[1]
    copies = []
    for t in range(2):
        cols = pl.ds(t * LANES, LANES)
        body = pl.ds(PAD, rows)
        copies += [
            (h_hbm.at[:, :, cols], h_ref.at[:, t, body, :]),
            (vel_hbm.at[0, :, :, cols], u_ref.at[:, t, body, :]),
            (vel_hbm.at[1, :, :, cols], v_ref.at[:, t, body, :]),
            (bot_hbm.at[:, cols], bc_ref.at[0, t, body, :]),
            (cor_hbm.at[:, cols], bc_ref.at[1, t, body, :]),
        ]
    copies = [pltpu.make_async_copy(s, d, sem.at[i]) for i, (s, d) in enumerate(copies)]
    for copy in copies:
        copy.start()
    for copy in copies:
        copy.wait()
    gx = lax.axis_index("gx")

    @pl.when(gx == lax.axis_size("gx") - 1)
    def _():
        lane = lane_iota((rows, LANES))
        for l in range(u_ref.shape[0]):
            edge = u_ref[l, 1, pl.ds(PAD, rows), :]
            u_ref[l, 1, pl.ds(PAD, rows), :] = jnp.where(lane == LANES - 1, 0.0, edge)

    even = gx % 2 == 0
    step = 16

    def chunk(k, carry):
        start = pl.multiple_of(k * step, step)
        span = (pl.multiple_of(start + PAD, 8), step)
        west = pack_side((h_ref, u_ref, v_ref), bc_ref, 0, 0, span)
        east = pack_side((h_ref, u_ref, v_ref), bc_ref, 1, LANES - 2, span)
        a_ref[pl.ds(start, step), :] = jnp.where(even, east, west)
        b_ref[pl.ds(start, step), :] = jnp.where(even, west, east)
        return carry

    lax.fori_loop(0, rows // step, chunk, 0)


def rows_kernel(h_ref, u_ref, v_ref, bc_ref, north_ref, south_ref):
    levels = h_ref.shape[0]
    rows = h_ref.shape[2] - 2 * PAD
    for t in range(2):
        cols = pl.ds(t * LANES, LANES)
        for f, ref in enumerate((h_ref, u_ref, v_ref)):
            for l in range(levels):
                spot = pl.ds(2 * (f * levels + l), 2)
                north_ref[spot, cols] = ref[l, t, pl.ds(PAD + rows - 2, 2), :]
                south_ref[spot, cols] = ref[l, t, pl.ds(PAD, 2), :]
        for f in range(2):
            spot = pl.ds(2 * (3 * levels + f), 2)
            north_ref[spot, cols] = bc_ref[f, t, pl.ds(PAD + rows - 2, 2), :]
            south_ref[spot, cols] = bc_ref[f, t, pl.ds(PAD, 2), :]


def corner_kernel(north_in, south_in, sa, sb, ra, rb, first_ref, second_ref):
    rows = sa.shape[0]
    even_x = lax.axis_index("gx") % 2 == 0
    even_y = lax.axis_index("gy") % 2 == 0

    def tail(start):
        span = pl.ds(start, 2)
        s1, s2, r1, r2 = sa[span, :], sb[span, :], ra[span, :], rb[span, :]
        return (
            jnp.where(even_x, r2, r1),
            jnp.where(even_x, r1, r2),
            jnp.where(even_x, s2, s1),
            jnp.where(even_x, s1, s2),
        )

    north, south = tail(rows - 2), tail(0)
    main = 52
    up, down = north_in[0:main, :], south_in[0:main, :]
    first_ref[0:main, :] = jnp.where(even_y, up, down)
    second_ref[0:main, :] = jnp.where(even_y, down, up)
    for i in range(4):
        spot = pl.ds(main + 2 * (i // 2), 2)
        cols = pl.ds(LANES * (i % 2), LANES)
        first_ref[spot, cols] = jnp.where(even_y, north[i], south[i])
        second_ref[spot, cols] = jnp.where(even_y, south[i], north[i])


def evaluate(fields, temps, height, spin, east, west, reduced, rows, step, update, keep=None, rates=True):
    h_ref, u_ref, v_ref = fields
    s_ref, fx_ref, fy_ref, b_ref, z_ref, vq_ref = temps

    def span(k, shift=0):
        return pl.ds(PAD + k * step + shift, step)

    def cells(k):
        h, hn = h_ref[:, span(k), :], h_ref[:, span(k, 1), :]
        u, un = u_ref[:, span(k), :], u_ref[:, span(k, 1), :]
        v, vs = v_ref[:, span(k), :], v_ref[:, span(k, -1), :]
        pair = h + east(h, "h", k)
        flux_x = 0.5 * pair * u
        flux_y = 0.5 * (h + hn) * v
        square = u * u
        kinetic = 0.25 * (square + west(square, "u2", k) + v * v + vs * vs)
        s_ref[:, span(k), :] = pair
        fx_ref[:, span(k), :] = flux_x
        fy_ref[:, span(k), :] = flux_y
        b_ref[:, span(k), :] = kinetic + (height(k) + reduced * h)
        z_ref[:, span(k), :] = (east(v, "v", k) - v) - (un - u) + spin(k)
        if keep is not None:
            keep[0][:, span(k), :] = square

    def finish(k):
        pair, pair_n = s_ref[:, span(k), :], s_ref[:, span(k, 1), :]
        fx, fxn = fx_ref[:, span(k), :], fx_ref[:, span(k, 1), :]
        fy, fys = fy_ref[:, span(k), :], fy_ref[:, span(k, -1), :]
        b, bn = b_ref[:, span(k), :], b_ref[:, span(k, 1), :]
        q = z_ref[:, span(k), :] / (0.25 * (pair + pair_n))
        uq = q * (0.5 * (fx + fxn))
        if keep is not None:
            keep[1][:, span(k), :] = uq
        if not rates:
            return
        vq = q * (0.5 * (fy + east(fy, "fy", k)))
        vq_ref[:, span(k), :] = vq
        dh = -((fx - west(fx, "fx", k)) + (fy - fys))
        dv = -0.5 * (west(uq, "uq", k) + uq) - (bn - b)
        du = 0.5 * (vq_ref[:, span(k, -1), :] + vq) - (east(b, "b", k) - b)
        update(k, dh, du, dv)

    count = rows // step
    cells(0)
    for k in range(count):
        if k + 1 < count:
            cells(k + 1)
        finish(k)


def group_sum(values):
    lane = lane_iota(values.shape)
    axis = values.ndim - 1
    for bit in (1, 2, 4):
        up = pltpu.roll(values, bit, axis)
        down = pltpu.roll(values, LANES - bit, axis)
        values = values + jnp.where((lane & bit) != 0, up, down)
    return values


def heun(rows, step, fields, bc, strips, reduced, gx, size_x, work, emit):
    mid, acc, strip_mid, strip_acc, height, temps, strip_temps, strip_keep = work
    levels = fields[0].shape[0]
    whole = pl.ds(PAD, rows)
    lane1 = lane_iota((1, step, LANES))
    lane2 = lane_iota((2, step, LANES))
    tile2 = lax.broadcasted_iota(jnp.int32, (2, step, LANES), 0)
    wall = jnp.where((tile2 == 1) & (lane2 == LANES - 1) & (gx == size_x - 1), 0.0, 1.0).astype(f32)
    edge_east, edge_west = lane1 == LANES - 1, lane1 == 0

    red_lane = jnp.zeros((1, 1, LANES), f32)
    lane0 = lane_iota((1, 1, LANES))
    for l in range(levels):
        red_lane = jnp.where((lane0 & 7) == l, reduced[l], red_lane)
    west_out = (lane1 < 16) & (gx == 0)
    east_out = (lane1 >= 48) & (gx == size_x - 1)
    out = west_out | east_out
    out_u = west_out | ((lane1 >= 40) & (gx == size_x - 1))

    def span(k):
        return pl.ds(PAD + k * step, step)

    def base(h_at):
        for k in range(rows // step):
            total = bc[0, :, span(k), :]
            for l in range(levels):
                total = total + h_at[l, :, span(k), :]
            height[:, span(k), :] = gravity * total

    def strip_stage(now, update, rates):
        def strip_height(k):
            return gravity * (strips[3, :, span(k), :] + group_sum(now[0, :, span(k), :]))

        evaluate(
            [now.at[i] for i in range(3)],
            [strip_temps.at[i] for i in range(6)],
            strip_height,
            lambda k: strips[4, :, span(k), :],
            lambda x, name, k: pltpu.roll(x, LANES - 8, 2),
            lambda x, name, k: pltpu.roll(x, 8, 2),
            red_lane, rows, step, update,
            keep=[strip_keep.at[0], strip_keep.at[1]], rates=rates,
        )

    def main_stage(now, strip_now, update):
        def one(l, carry):
            inject = {
                "h": strip_now.at[0], "v": strip_now.at[2],
                "fx": strip_temps.at[1], "fy": strip_temps.at[2], "b": strip_temps.at[3],
                "u2": strip_keep.at[0], "uq": strip_keep.at[1],
            }

            def east(x, name, k):
                moved = pltpu.roll(x, LANES - 1, 2)
                edge = pltpu.roll(inject[name][:, span(k), :], 79 - l, 2)
                return jnp.concatenate(
                    [
                        jnp.where(edge_east, moved[1:2], moved[0:1]),
                        jnp.where(edge_east, edge, moved[1:2]),
                    ],
                    axis=0,
                )

            def west(x, name, k):
                moved = pltpu.roll(x, 1, 2)
                edge = pltpu.roll(inject[name][:, span(k), :], 120 - l, 2)
                return jnp.concatenate(
                    [
                        jnp.where(edge_west, edge, moved[0:1]),
                        jnp.where(edge_west, moved[0:1], moved[1:2]),
                    ],
                    axis=0,
                )

            evaluate(
                [ref.at[l] for ref in now],
                [temps.at[i] for i in range(6)],
                lambda k: height[:, span(k), :],
                lambda k: bc[1, :, span(k), :],
                east, west, reduced[l], rows, step,
                lambda k, dh, du, dv: update(l, k, dh, du, dv),
            )
            return carry

        lax.fori_loop(0, levels, one, 0)

    def strip_first(k, dh, du, dv):
        for i, (rate, mask) in enumerate(((dh, out), (du, out_u), (dv, out))):
            value = strips[i, :, span(k), :] + time_step * rate
            strip_mid[i, :, span(k), :] = jnp.where(mask, 0.0, value)

    strip_stage(strips, strip_first, True)
    base(fields[0])

    def first(l, k, dh, du, dv):
        for i, rate in enumerate((dh, du, dv)):
            start = fields[i][l, :, span(k), :]
            value = start + time_step * rate
            if i == 1:
                value = value * wall
            mid[i, l, :, span(k), :] = value
            acc[i, l, :, pl.ds(k * step, step), :] = start + half_step * rate

    main_stage(fields, strips, first)

    strip_stage(strip_mid, None, False)
    base(mid.at[0])

    def second(l, k, dh, du, dv):
        for i, rate in enumerate((dh, du, dv)):
            value = acc[i, l, :, pl.ds(k * step, step), :] + half_step * rate
            if i == 1:
                value = value * wall
            emit(i, l, k, value)

    main_stage([mid.at[i] for i in range(3)], strip_mid, second)


def work_shapes(levels, rows):
    total = rows + 2 * PAD
    return [
        VM((3, levels, 2, total, LANES), f32),
        VM((3, levels, 2, rows, LANES), f32),
        VM((3, 1, total, LANES), f32),
        VM((1, 8, LANES), f32),
        VM((2, total, LANES), f32),
        VM((6, 2, total, LANES), f32),
        VM((6, 1, total, LANES), f32),
        VM((2, 1, total, LANES), f32),
    ]


def build_strips(strips, sources, rows):
    lane = lane_iota((rows, LANES))
    for f in range(5):
        value = jnp.zeros((rows, LANES), f32)
        for g, item in enumerate(sources):
            moved = pltpu.roll(item, (16 * g - 16 * f) % LANES, 1)
            value = jnp.where((lane >= 16 * g) & (lane < 16 * g + 16), moved, value)
        strips[f, 0, pl.ds(PAD, rows), :] = value


def inner_kernel(h_ref, u_ref, v_ref, bc_ref, sa, sb, ra, rb, reduced, h_out, vel_out, edge_ref, strips, result, sem, *work):
    gx, size_x = lax.axis_index("gx"), lax.axis_size("gx")
    levels = h_ref.shape[0]
    rows = h_ref.shape[2] - 2 * PAD
    even = gx % 2 == 0
    s1, s2, r1, r2 = sa[...], sb[...], ra[...], rb[...]
    build_strips(
        strips,
        (jnp.where(even, r2, r1), jnp.where(even, s2, s1), jnp.where(even, s1, s2), jnp.where(even, r1, r2)),
        rows,
    )
    step = 8
    last = rows // step - 1

    def emit(i, l, k, value):
        if k == 0 or k == last:
            edge_ref[i, l, :, pl.ds(0 if k == 0 else step, step), :] = value
        else:
            result[i, l, :, pl.ds(k * step, step), :] = value

    heun(rows, step, (h_ref, u_ref, v_ref), bc_ref, strips, reduced, gx, size_x, work, emit)
    body = pl.ds(step, rows - 2 * step)
    copies = []
    for t in range(2):
        cols = pl.ds(t * LANES, LANES)
        copies += [
            (result.at[0, :, t, body, :], h_out.at[:, body, cols]),
            (result.at[1, :, t, body, :], vel_out.at[0, :, body, cols]),
            (result.at[2, :, t, body, :], vel_out.at[1, :, body, cols]),
        ]
    copies = [pltpu.make_async_copy(s, d, sem.at[i]) for i, (s, d) in enumerate(copies)]
    for copy in copies:
        copy.start()
    for copy in copies:
        copy.wait()


def outer_kernel(h_ref, u_ref, v_ref, bc_ref, sa, sb, ra, rb, m0, m1, reduced, edge_in, h_in, vel_in,
                 h_out, vel_out, own, bc, strips, sides, result, sem, *work):
    gx, size_x = lax.axis_index("gx"), lax.axis_size("gx")
    levels = h_ref.shape[0]
    rows = h_ref.shape[2] - 2 * PAD
    even_x = gx % 2 == 0
    even_y = lax.axis_index("gy") % 2 == 0
    top, bottom = PAD, PAD + 8

    first, second = m0[...], m1[...]
    north = jnp.where(even_y, first, second)
    south = jnp.where(even_y, second, first)

    def place(dst, index, src, spot, t):
        dst[(*index, pl.ds(top, 2), slice(None))] = south[spot : spot + 2, t * LANES : (t + 1) * LANES]
        dst[(*index, pl.ds(top + 2, 6), slice(None))] = src[0]
        dst[(*index, pl.ds(bottom, 6), slice(None))] = src[1]
        dst[(*index, pl.ds(bottom + 6, 2), slice(None))] = north[spot : spot + 2, t * LANES : (t + 1) * LANES]

    low, high = pl.ds(PAD, 6), pl.ds(PAD + rows - 6, 6)
    for t in range(2):
        for f, ref in enumerate((h_ref, u_ref, v_ref)):
            for l in range(levels):
                place(own, (f, l, t), (ref[l, t, low, :], ref[l, t, high, :]), 2 * (f * levels + l), t)
        for f in range(2):
            place(bc, (f, t), (bc_ref[f, t, low, :], bc_ref[f, t, high, :]), 2 * (3 * levels + f), t)

    def pick(a, b, span):
        return jnp.where(even_x, a[span, :], b[span, :])

    low, high = pl.ds(0, 6), pl.ds(rows - 6, 6)
    for i, (a, b) in enumerate(((rb, ra), (sb, sa), (sa, sb), (ra, rb))):
        spot, t = ((52, 0), (54, 0), (54, 1), (52, 1))[i]
        place(sides, (i,), (pick(a, b, low), pick(a, b, high)), spot, t)
    build_strips(strips, [sides[i, pl.ds(PAD, 16), :] for i in range(4)], 16)

    result[...] = edge_in[...]

    def emit(i, l, k, value):
        result[i, l, :, pl.ds(0, 2), :] = value[:, 2:4, :]
        result[i, l, :, pl.ds(14, 2), :] = value[:, 12:14, :]

    heun(16, 16, [own.at[i] for i in range(3)], bc, strips, reduced, gx, size_x, work, emit)
    copies = []
    for t in range(2):
        cols = pl.ds(t * LANES, LANES)
        for part, start in ((0, 0), (1, rows - 8)):
            src, dst = pl.ds(8 * part, 8), pl.ds(start, 8)
            copies += [
                (result.at[0, :, t, src, :], h_out.at[:, dst, cols]),
                (result.at[1, :, t, src, :], vel_out.at[0, :, dst, cols]),
                (result.at[2, :, t, src, :], vel_out.at[1, :, dst, cols]),
            ]
    copies = [pltpu.make_async_copy(s, d, sem.at[i]) for i, (s, d) in enumerate(copies)]
    for copy in copies:
        copy.start()
    for copy in copies:
        copy.wait()


def body(thickness, velocity, bottom, coriolis, reduced):
    levels, rows, columns = thickness.shape
    total = rows + 2 * PAD
    field = VM((levels, 2, total, LANES), f32)
    message_x, message_y = VM((rows, LANES), f32), VM((56, 2 * LANES), f32)

    def exchange(values, axis, periodic):
        count = lax.axis_size(axis)
        return [lax.ppermute(item, axis, swap_pairs(count, i, periodic)) for i, item in enumerate(values)]

    h, u, v, bc, sa, sb = pin(pl.pallas_call(
        load_kernel,
        out_shape=[field, field, field, VM((2, 2, total, LANES), f32), message_x, message_x],
        in_specs=[ASPEC] * 4,
        out_specs=[VSPEC] * 6,
        scratch_shapes=[pltpu.SemaphoreType.DMA((10,))],
        name="load",
    )(thickness, velocity, bottom, coriolis))
    ra, rb = pin(exchange((sa, sb), "gx", False))
    north, south = pin(pl.pallas_call(
        rows_kernel,
        out_shape=[message_y, message_y],
        in_specs=[VSPEC] * 4,
        out_specs=[VSPEC] * 2,
        name="edges",
    )(h, u, v, bc))
    y0, y1 = pin(pl.pallas_call(
        corner_kernel,
        out_shape=[message_y, message_y],
        in_specs=[VSPEC] * 6,
        out_specs=[VSPEC] * 2,
        name="corners",
    )(north, south, sa, sb, ra, rb))
    m0, m1 = pin(exchange((y0, y1), "gy", True))

    h_mid, vel_mid, edge = pl.pallas_call(
        inner_kernel,
        out_shape=[
            jax.ShapeDtypeStruct(thickness.shape, f32),
            jax.ShapeDtypeStruct(velocity.shape, f32),
            VM((3, levels, 2, 16, LANES), f32),
        ],
        in_specs=[VSPEC] * 8 + [SSPEC],
        out_specs=[ASPEC, ASPEC, VSPEC],
        scratch_shapes=[
            VM((5, 1, total, LANES), f32),
            VM((3, levels, 2, rows, LANES), f32),
            pltpu.SemaphoreType.DMA((6,)),
            *work_shapes(levels, rows),
        ],
        name="inner",
    )(h, u, v, bc, sa, sb, ra, rb, reduced)
    (edge,) = pin([edge])
    return tuple(pl.pallas_call(
        outer_kernel,
        out_shape=[
            jax.ShapeDtypeStruct(thickness.shape, f32),
            jax.ShapeDtypeStruct(velocity.shape, f32),
        ],
        in_specs=[VSPEC] * 10 + [SSPEC, VSPEC, ASPEC, ASPEC],
        out_specs=[ASPEC, ASPEC],
        input_output_aliases={12: 0, 13: 1},
        scratch_shapes=[
            VM((3, levels, 2, 32, LANES), f32),
            VM((2, 2, 32, LANES), f32),
            VM((5, 1, 32, LANES), f32),
            VM((4, 32, LANES), f32),
            VM((3, levels, 2, 16, LANES), f32),
            pltpu.SemaphoreType.DMA((12,)),
            *work_shapes(levels, 16),
        ],
        name="outer",
    )(h, u, v, bc, sa, sb, ra, rb, m0, m1, reduced, edge, h_mid, vel_mid))


def solution(mesh):
    return jax.shard_map(
        body,
        mesh=mesh,
        in_specs=(
            P(None, "gy", "gx"),
            P(None, None, "gy", "gx"),
            P("gy", "gx"),
            P("gy", "gx"),
            P(),
        ),
        out_specs=(P(None, "gy", "gx"), P(None, None, "gy", "gx")),
        check_vma=False,
    )
```

```python
import jax
import jax.numpy as jnp
from jax import lax
from jax.experimental import pallas as pl
from jax.experimental.pallas import tpu as pltpu
from jax.sharding import PartitionSpec as P


gravity = 0.5
time_step = 0.1
half_step = 0.05
PAD = 8
LANES = 128
SMALL, LARGE = 4 << 20, 16 << 20
MAIN = 52
UNROLL = 1
f32 = jnp.float32
VM = pltpu.VMEM
VSPEC = pl.BlockSpec(memory_space=pltpu.VMEM)
ASPEC = pl.BlockSpec(memory_space=pl.ANY)
SSPEC = pl.BlockSpec(memory_space=pltpu.SMEM)


def lane_iota(shape):
    return lax.broadcasted_iota(jnp.int32, shape, len(shape) - 1)


def pin(values, space=pltpu.VMEM):
    return [pltpu.with_memory_space_constraint(item, space) for item in values]


def swap_pairs(count, first, periodic):
    pairs = []
    for low in range(first, count, 2):
        high = low + 1
        if high >= count:
            if not periodic:
                continue
            high -= count
        pairs += [(low, high), (high, low)]
    return pairs


GROUPS = 12
EAST_HALO = 8 * (GROUPS - 2)


def permute_lanes(values, index):
    return jnp.take_along_axis(values, index, axis=1, mode="promise_in_bounds")


def own_columns(refs, rows):
    lane = lane_iota((rows[1], LANES))
    group = lane >> 3
    west_index = jnp.clip(group - 2, 0, LANES - 1)
    east_index = jnp.clip(group + (LANES - 10), 0, LANES - 1)
    west = jnp.zeros((rows[1], LANES), f32)
    east = jnp.zeros((rows[1], LANES), f32)
    for l, (first, second) in enumerate(refs):
        moved_west = permute_lanes(first[pl.ds(*rows), :], west_index)
        moved_east = permute_lanes(second[pl.ds(*rows), :], east_index)
        mine = (lane & 7) == l if len(refs) > 1 else lane >= 0
        west = jnp.where(mine, moved_west, west)
        east = jnp.where(mine, moved_east, east)
    both = jnp.where(lane < 48, west, east)
    return jnp.where((lane >= 16) & (lane < EAST_HALO), both, 0.0)


def join_strip(own, from_west, from_east, f):
    lane = lane_iota(own.shape)
    west = pltpu.roll(from_west, (-16 * f) % LANES, 1)
    east = pltpu.roll(from_east, (EAST_HALO - 16 * f) % LANES, 1)
    value = jnp.where(lane < 16, west, own)
    return jnp.where((lane >= EAST_HALO) & (lane < EAST_HALO + 16), east, value)


def load_kernel(h_hbm, vel_hbm, bot_hbm, cor_hbm, red_hbm, h_ref, u_ref, v_ref, bc_ref, own_ref, a_ref, b_ref, red_ref, red, sem):
    levels, rows = h_hbm.shape[0], h_hbm.shape[1]
    copies = []
    for t in range(2):
        cols = pl.ds(t * LANES, LANES)
        body = pl.ds(PAD, rows)
        copies += [
            (h_hbm.at[:, :, cols], h_ref.at[:, t, body, :]),
            (vel_hbm.at[0, :, :, cols], u_ref.at[:, t, body, :]),
            (vel_hbm.at[1, :, :, cols], v_ref.at[:, t, body, :]),
            (bot_hbm.at[:, cols], bc_ref.at[0, t, body, :]),
            (cor_hbm.at[:, cols], bc_ref.at[1, t, body, :]),
        ]
    copies = [pltpu.make_async_copy(s, d, sem.at[i]) for i, (s, d) in enumerate(copies)]
    few = pltpu.make_async_copy(red_hbm, red, sem.at[10])
    for i in (0, 5, 1, 6, 2, 7, 3, 8, 4, 9):
        copies[i].start()
    few.start()
    gx = lax.axis_index("gx")
    even = gx % 2 == 0
    step = 32
    lane = lane_iota((step, LANES))

    for f in range(5):
        copies[f].wait()
        copies[5 + f].wait()
        if f == 1:
            @pl.when(gx == lax.axis_size("gx") - 1)
            def _():
                lane = lane_iota((rows, LANES))
                for l in range(levels):
                    edge = u_ref[l, 1, pl.ds(PAD, rows), :]
                    u_ref[l, 1, pl.ds(PAD, rows), :] = jnp.where(lane == LANES - 1, 0.0, edge)

        for k in range(rows // step):
            if f < 3:
                ref = (h_ref, u_ref, v_ref)[f]
                refs = [(ref.at[l, 0], ref.at[l, 1]) for l in range(levels)]
            else:
                refs = [(bc_ref.at[f - 3, 0], bc_ref.at[f - 3, 1])]
            own_ref[f, 0, pl.ds(PAD + k * step, step), :] = own_columns(refs, (PAD + k * step, step))
    for k in range(rows // step):
        west = jnp.zeros((step, LANES), f32)
        east = jnp.zeros((step, LANES), f32)
        for f in range(5):
            own = own_ref[f, 0, pl.ds(PAD + k * step, step), :]
            mine = (lane >= 16 * f) & (lane < 16 * f + 16)
            west = jnp.where(mine, pltpu.roll(own, (16 * f - 16) % LANES, 1), west)
            east = jnp.where(mine, pltpu.roll(own, (16 * f - 64) % LANES, 1), east)
        a_ref[pl.ds(k * step, step), :] = jnp.where(even, east, west)
        b_ref[pl.ds(k * step, step), :] = jnp.where(even, west, east)
    few.wait()
    for l in range(levels):
        red_ref[pl.ds(l, 1), :] = jnp.full((1, LANES), red[l], f32)


def rows_kernel(h_ref, u_ref, v_ref, bc_ref, north_ref, south_ref, own, bc):
    levels = h_ref.shape[0]
    rows = h_ref.shape[2] - 2 * PAD
    low, high = pl.ds(PAD, 6), pl.ds(PAD + rows - 6, 6)
    for src, dst in ((h_ref, own.at[0]), (u_ref, own.at[1]), (v_ref, own.at[2]), (bc_ref, bc)):
        for l in range(src.shape[0]):
            dst[l, :, pl.ds(PAD + 2, 6), :] = src[l, :, low, :]
            dst[l, :, pl.ds(PAD + 8, 6), :] = src[l, :, high, :]
    for t in range(2):
        cols = pl.ds(t * LANES, LANES)
        for f, ref in enumerate((h_ref, u_ref, v_ref)):
            for l in range(levels):
                spot = pl.ds(2 * (f * levels + l), 2)
                north_ref[spot, cols] = ref[l, t, pl.ds(PAD + rows - 2, 2), :]
                south_ref[spot, cols] = ref[l, t, pl.ds(PAD, 2), :]
        for f in range(2):
            spot = pl.ds(2 * (3 * levels + f), 2)
            north_ref[spot, cols] = bc_ref[f, t, pl.ds(PAD + rows - 2, 2), :]
            south_ref[spot, cols] = bc_ref[f, t, pl.ds(PAD, 2), :]


def corner_kernel(north_in, south_in, own_ref, ra, rb, after, first_ref, second_ref):
    rows = ra.shape[0]
    even_x = lax.axis_index("gx") % 2 == 0
    even_y = lax.axis_index("gy") % 2 == 0
    up, down = north_in[0:MAIN, :], south_in[0:MAIN, :]
    first_ref[0:MAIN, :] = jnp.where(even_y, up, down)
    second_ref[0:MAIN, :] = jnp.where(even_y, down, up)

    def tail(start, f):
        span = pl.ds(start, 8)
        r1, r2 = ra[span, :], rb[span, :]
        own = own_ref[f, 0, pl.ds(PAD + start, 8), :]
        return join_strip(own, jnp.where(even_x, r2, r1), jnp.where(even_x, r1, r2), f)

    for f in range(5):
        north, south = tail(rows - 8, f), tail(0, f)
        for r in range(2):
            cols = pl.ds(LANES * r, LANES)
            up, down = north[6 + r : 7 + r, :], south[r : r + 1, :]
            first_ref[pl.ds(MAIN + f, 1), cols] = jnp.where(even_y, up, down)
            second_ref[pl.ds(MAIN + f, 1), cols] = jnp.where(even_y, down, up)


def evaluate(fields, temps, height, spin, east, west, reduced, rows, step, update):
    h_ref, u_ref, v_ref = fields
    s_ref, fx_ref, fy_ref, b_ref, z_ref, vq_ref = temps

    def span(k, shift=0):
        return pl.ds(PAD + k * step + shift, step)

    def cells(k):
        h, hn = h_ref[:, span(k), :], h_ref[:, span(k, 1), :]
        u, un = u_ref[:, span(k), :], u_ref[:, span(k, 1), :]
        v, vs = v_ref[:, span(k), :], v_ref[:, span(k, -1), :]
        pair = h + east(h)
        square = u * u
        kinetic = 0.25 * (square + west(square) + v * v + vs * vs)
        s_ref[:, span(k), :] = pair
        fx_ref[:, span(k), :] = 0.5 * pair * u
        fy_ref[:, span(k), :] = 0.5 * (h + hn) * v
        b_ref[:, span(k), :] = kinetic + (height(k) + reduced * h)
        z_ref[:, span(k), :] = (east(v) - v) - (un - u) + spin(k)

    def finish(k):
        pair, pair_n = s_ref[:, span(k), :], s_ref[:, span(k, 1), :]
        fx, fxn = fx_ref[:, span(k), :], fx_ref[:, span(k, 1), :]
        fy, fys = fy_ref[:, span(k), :], fy_ref[:, span(k, -1), :]
        b, bn = b_ref[:, span(k), :], b_ref[:, span(k, 1), :]
        q = z_ref[:, span(k), :] / (0.25 * (pair + pair_n))
        uq = q * (0.5 * (fx + fxn))
        vq = q * (0.5 * (fy + east(fy)))
        vq_ref[:, span(k), :] = vq
        dh = -((fx - west(fx)) + (fy - fys))
        dv = -0.5 * (west(uq) + uq) - (bn - b)
        du = 0.5 * (vq_ref[:, span(k, -1), :] + vq) - (east(b) - b)
        update(k, dh, du, dv)

    count = rows // step
    cells(0)
    for k in range(count):
        if k + 1 < count:
            cells(k + 1)
        finish(k)


def span_of(k, step):
    return pl.ds(PAD + k * step, step)


def group_sum(values):
    lane = lane_iota(values.shape)
    axis = values.ndim - 1
    for bit in (1, 2, 4):
        up = pltpu.roll(values, bit, axis)
        down = pltpu.roll(values, LANES - bit, axis)
        values = values + jnp.where((lane & bit) != 0, up, down)
    return values


def base(h_at, bc, height, rows, step):
    for k in range(rows // step):
        total = bc[0, :, span_of(k, step), :]
        for l in range(h_at.shape[0]):
            total = total + h_at[l, :, span_of(k, step), :]
        height[:, span_of(k, step), :] = gravity * total


def main_stage(now, temps, height, bc, reduced, rows, step, unroll, update, after=None):
    lane = lane_iota((1, step, LANES))

    def east(x):
        moved = pltpu.roll(x, LANES - 1, 2)
        return jnp.concatenate([jnp.where(lane == LANES - 1, moved[1:2], moved[0:1]), moved[1:2]], axis=0)

    def west(x):
        moved = pltpu.roll(x, 1, 2)
        return jnp.concatenate([moved[0:1], jnp.where(lane == 0, moved[0:1], moved[1:2])], axis=0)

    def one(l, slot):
        evaluate(
            [ref.at[l] for ref in now],
            [temps.at[slot, i] for i in range(6)],
            lambda k: height[:, span_of(k, step), :],
            lambda k: bc[1, :, span_of(k, step), :],
            east, west, reduced[pl.ds(l, 1), :][None], rows, step,
            lambda k, dh, du, dv: update(l, k, (dh, du, dv)),
        )
        if after is not None:
            after(l)

    levels = now[0].shape[0]

    def some(j, carry):
        for slot in range(unroll):
            one(j * unroll + slot, slot)
        return carry

    if unroll == levels:
        some(0, 0)
    else:
        lax.fori_loop(0, levels // unroll, some, 0)


def strip_stages(strips, mid, acc, temps, reduced, gx, size_x, rows, step):
    lane = lane_iota((1, step, LANES))
    west_out = (lane < 16) & (gx == 0)
    out = west_out | ((lane >= EAST_HALO) & (gx == size_x - 1))
    out_u = west_out | ((lane >= EAST_HALO - 8) & (gx == size_x - 1))
    small = lane_iota((1, 1, LANES))
    red_lane = jnp.zeros((1, 1, LANES), f32)
    for l in range(8):
        red_lane = jnp.where((small & 7) == l, reduced[l : l + 1, :][None], red_lane)

    def stage(now, update):
        def height(k):
            return gravity * (strips[3, :, span_of(k, step), :] + group_sum(now[0, :, span_of(k, step), :]))

        evaluate(
            [now.at[i] for i in range(3)],
            [temps.at[i] for i in range(6)],
            height,
            lambda k: strips[4, :, span_of(k, step), :],
            lambda x: pltpu.roll(x, LANES - 8, 2),
            lambda x: pltpu.roll(x, 8, 2),
            red_lane, rows, step, update,
        )

    def first(k, *rates):
        for i, rate in enumerate(rates):
            start = strips[i, :, span_of(k, step), :]
            mid[i, :, span_of(k, step), :] = jnp.where(out_u if i == 1 else out, 0.0, start + time_step * rate)
            acc[i, :, span_of(k, step), :] = start + half_step * rate

    def second(k, *rates):
        for i, rate in enumerate(rates):
            value = acc[i, :, span_of(k, step), :] + half_step * rate
            acc[i, :, span_of(k, step), :] = jnp.where(out_u, 0.0, value) if i == 1 else value

    stage(strips, first)
    stage(mid, second)


def first_update(fields, mid, acc, step):
    def update(l, k, rates):
        for i, rate in enumerate(rates):
            start = fields[i][l, :, span_of(k, step), :]
            mid[i, l, :, span_of(k, step), :] = start + time_step * rate
            acc[i, l, :, pl.ds(k * step, step), :] = start + half_step * rate

    return update


def second_update(acc, strip, step, emit):
    lane = lane_iota((step, LANES))
    index = jnp.where(lane < 64, 16 + 8 * lane, 64 + 8 * (lane - (LANES - 2)))
    index = jnp.where((lane < 2) | (lane >= LANES - 2), index, 0)

    def update(l, k, rates):
        for i, rate in enumerate(rates):
            value = acc[i, l, :, pl.ds(k * step, step), :] + half_step * rate
            edge = permute_lanes(strip[i, 0, span_of(k, step), :], index + l)
            emit(i, l, k, jnp.where(lane < 2, edge, value[0]), jnp.where(lane >= LANES - 2, edge, value[1]))

    return update


def first_kernel(h_ref, u_ref, v_ref, bc_ref, reduced, mid, acc, height, temps):
    rows = h_ref.shape[2] - 2 * PAD
    step = 8
    base(h_ref, bc_ref, height, rows, step)
    main_stage((h_ref, u_ref, v_ref), temps, height, bc_ref, reduced, rows, step, UNROLL,
               first_update((h_ref, u_ref, v_ref), mid, acc, step))


def second_kernel(own_ref, ra, rb, mid, acc, bc_ref, reduced, h_out, vel_out, edge_ref, strip_ref,
                  result, sem, strip_mid, strip_acc, height, temps, strip_temps):
    gx, size_x = lax.axis_index("gx"), lax.axis_size("gx")
    rows = ra.shape[0]
    even_x = gx % 2 == 0
    r1, r2 = ra[...], rb[...]
    from_west, from_east = jnp.where(even_x, r2, r1), jnp.where(even_x, r1, r2)
    for f in range(5):
        strip_ref[f, 0, pl.ds(PAD, rows), :] = join_strip(own_ref[f, 0, pl.ds(PAD, rows), :], from_west, from_east, f)
    step = 8
    last = rows // step - 1
    strip_stages(strip_ref, strip_mid, strip_acc, strip_temps, reduced, gx, size_x, rows, 16)
    base(mid.at[0], bc_ref, height, rows, step)

    def emit(i, l, k, *tiles):
        for t, value in enumerate(tiles):
            if k == 0 or k == last:
                edge_ref[i, l, t, pl.ds(0 if k == 0 else step, step), :] = value
            else:
                result[i, l, t, pl.ds(k * step, step), :] = value

    body = pl.ds(step, rows - 2 * step)
    levels = mid.shape[1]

    def copies(l):
        out = []
        for t in range(2):
            cols = pl.ds(t * LANES, LANES)
            for i, target in enumerate((h_out.at[l], vel_out.at[0, l], vel_out.at[1, l])):
                source = result.at[i, l, t, body, :]
                out.append(pltpu.make_async_copy(source, target.at[body, cols], sem.at[l, 3 * t + i]))
        return out

    main_stage([mid.at[i] for i in range(3)], temps, height, bc_ref, reduced, rows, step, UNROLL,
               second_update(acc, strip_acc, step, emit), lambda l: [copy.start() for copy in copies(l)])

    def finish(l, carry):
        for copy in copies(l):
            copy.wait()
        return carry

    lax.fori_loop(0, levels, finish, 0)


def store(result, h_out, vel_out, sem, spans):
    copies = []
    for t in range(2):
        cols = pl.ds(t * LANES, LANES)
        for src, dst in spans:
            copies += [
                (result.at[0, :, t, src, :], h_out.at[:, dst, cols]),
                (result.at[1, :, t, src, :], vel_out.at[0, :, dst, cols]),
                (result.at[2, :, t, src, :], vel_out.at[1, :, dst, cols]),
            ]
    copies = [pltpu.make_async_copy(s, d, sem.at[i]) for i, (s, d) in enumerate(copies)]
    for copy in copies:
        copy.start()
    for copy in copies:
        copy.wait()


def outer_kernel(strip_ref, m0, m1, reduced, own_in, bc_in, edge_in, h_in, vel_in,
                 h_out, vel_out, own, bc, result, strips, mid, acc, sem, strip_mid, strip_acc, height, temps, strip_temps):
    gx, size_x = lax.axis_index("gx"), lax.axis_size("gx")
    levels = own.shape[1]
    rows = h_out.shape[1]
    even_y = lax.axis_index("gy") % 2 == 0
    top, bottom = PAD, PAD + 8
    low, high = pl.ds(PAD, 6), pl.ds(PAD + rows - 6, 6)

    first, second = m0[...], m1[...]
    north = jnp.where(even_y, first, second)
    south = jnp.where(even_y, second, first)

    for t in range(2):
        cols = slice(t * LANES, (t + 1) * LANES)

        def place(dst, index, spot):
            dst[(*index, t, pl.ds(top, 2), slice(None))] = south[spot : spot + 2, cols]
            dst[(*index, t, pl.ds(bottom + 6, 2), slice(None))] = north[spot : spot + 2, cols]

        for f in range(3):
            for l in range(levels):
                place(own, (f, l), 2 * (f * levels + l))
        for f in range(2):
            place(bc, (f,), 2 * (3 * levels + f))
    for f in range(5):
        for r in range(2):
            cols = slice(r * LANES, (r + 1) * LANES)
            strips[f, 0, pl.ds(top + r, 1), :] = south[MAIN + f : MAIN + f + 1, cols]
            strips[f, 0, pl.ds(bottom + 6 + r, 1), :] = north[MAIN + f : MAIN + f + 1, cols]
        strips[f, 0, pl.ds(top + 2, 6), :] = strip_ref[f, 0, low, :]
        strips[f, 0, pl.ds(bottom, 6), :] = strip_ref[f, 0, high, :]

    strip_stages(strips, strip_mid, strip_acc, strip_temps, reduced, gx, size_x, 16, 16)
    fields = [own.at[i] for i in range(3)]
    base(fields[0], bc, height, 16, 16)
    main_stage(fields, temps, height, bc, reduced, 16, 16, levels, first_update(fields, mid, acc, 16))
    base(mid.at[0], bc, height, 16, 16)
    def emit(i, l, k, *tiles):
        for t, value in enumerate(tiles):
            result[i, l, t, pl.ds(0, 2), :] = value[2:4, :]
            result[i, l, t, pl.ds(14, 2), :] = value[12:14, :]

    main_stage([mid.at[i] for i in range(3)], temps, height, bc, reduced, 16, 16, levels,
               second_update(acc, strip_acc, 16, emit))
    store(result, h_out, vel_out, sem, ((pl.ds(0, 8), pl.ds(0, 8)), (pl.ds(8, 8), pl.ds(rows - 8, 8))))


def work_shapes(rows, unroll):
    total = rows + 2 * PAD
    return [
        VM((3, 1, total, LANES), f32),
        VM((3, 1, total, LANES), f32),
        VM((2, total, LANES), f32),
        VM((unroll, 6, 2, total, LANES), f32),
        VM((6, 1, total, LANES), f32),
    ]


def body(thickness, velocity, bottom, coriolis, reduced):
    levels, rows, columns = thickness.shape
    total = rows + 2 * PAD
    field = VM((levels, 2, total, LANES), f32)
    strip = VM((5, 1, total, LANES), f32)
    message_x, message_y = VM((rows, LANES), f32), VM((64, 2 * LANES), f32)
    h_shape = jax.ShapeDtypeStruct(thickness.shape, f32)
    vel_shape = jax.ShapeDtypeStruct(velocity.shape, f32)
    edge_shape = VM((3, levels, 2, 16, LANES), f32)

    def call(kernel, name, out_shape, in_specs, args, out_specs=None, scratch=(), limit=SMALL, aliases={}):
        return pl.pallas_call(
            kernel,
            out_shape=out_shape,
            in_specs=in_specs,
            out_specs=out_specs or [VSPEC] * len(out_shape),
            scratch_shapes=list(scratch),
            input_output_aliases=aliases,
            compiler_params=pltpu.CompilerParams(vmem_limit_bytes=limit),
            name=name,
        )(*args)

    size_x, size_y = lax.axis_size("gx"), lax.axis_size("gy")

    args = pin((thickness, velocity, bottom, coriolis, reduced), pltpu.HBM)
    h, u, v, bc, own, sa, sb, red = pin(call(
        load_kernel, "load",
        [field, field, field, VM((2, 2, total, LANES), f32), strip, message_x, message_x, VM((levels, LANES), f32)],
        [ASPEC] * 5, args, scratch=[pltpu.SMEM((levels,), f32), pltpu.SemaphoreType.DMA((11,))],
    ))
    ra, rb = pin([lax.ppermute(item, "gx", swap_pairs(size_x, i, False)) for i, item in enumerate((sa, sb))])
    edge_fields, edge_fixed = VM((3, levels, 2, 32, LANES), f32), VM((2, 2, 32, LANES), f32)
    north, south, own_edge, bc_edge = pin(call(
        rows_kernel, "edges", [message_y] * 2 + [edge_fields, edge_fixed], [VSPEC] * 4, (h, u, v, bc),
    ))
    mid, acc = pin(call(
        first_kernel, "first",
        [VM((3, levels, 2, total, LANES), f32), VM((3, levels, 2, rows, LANES), f32)],
        [VSPEC] * 5, (h, u, v, bc, red),
        scratch=[VM((2, total, LANES), f32), VM((UNROLL, 6, 2, total, LANES), f32)],
    ))
    y0, y1 = pin(call(
        corner_kernel, "corners", [message_y] * 2, [VSPEC] * 6, (north, south, own, ra, rb, mid),
    ))
    m0, m1 = pin([lax.ppermute(item, "gy", swap_pairs(size_y, i, True)) for i, item in enumerate((y0, y1))])
    work = [VM((3, levels, 2, rows, LANES), f32), pltpu.SemaphoreType.DMA((levels, 6)), *work_shapes(rows, UNROLL)]
    h_new, vel_new, edge, strips = call(
        second_kernel, "second", [h_shape, vel_shape, edge_shape, strip], [VSPEC] * 7,
        (own, ra, rb, mid, acc, bc, red), [ASPEC, ASPEC, VSPEC, VSPEC], work, LARGE,
    )
    edge, strips = pin([edge, strips])
    return tuple(call(
        outer_kernel, "outer", [h_shape, vel_shape, edge_fields, edge_fixed, edge_shape],
        [VSPEC] * 7 + [ASPEC, ASPEC],
        (strips, m0, m1, red, own_edge, bc_edge, edge, h_new, vel_new),
        [ASPEC, ASPEC, VSPEC, VSPEC, VSPEC],
        [
            VM((5, 1, 32, LANES), f32),
            VM((3, levels, 2, 32, LANES), f32),
            VM((3, levels, 2, 16, LANES), f32),
            pltpu.SemaphoreType.DMA((12,)),
            *work_shapes(16, levels),
        ],
        LARGE, {7: 0, 8: 1, 4: 2, 5: 3, 6: 4},
    )[:2])


def solution(mesh):
    return jax.shard_map(
        body,
        mesh=mesh,
        in_specs=(
            P(None, "gy", "gx"),
            P(None, None, "gy", "gx"),
            P("gy", "gx"),
            P("gy", "gx"),
            P(),
        ),
        out_specs=(P(None, "gy", "gx"), P(None, None, "gy", "gx")),
        check_vma=False,
    )
```

```python
import jax
import jax.numpy as jnp
from jax import lax
from jax.experimental import pallas as pl
from jax.experimental.pallas import tpu as pltpu
from jax.sharding import PartitionSpec as P


time_step = 0.1
half_step = 0.05
PAD = 8
LANES = 128
SMALL, LARGE = 4 << 20, 16 << 20
MAIN = 52
UNROLL = 1
RATE = (-0.5, 0.5, -0.5)
f32 = jnp.float32
VM = pltpu.VMEM
VSPEC = pl.BlockSpec(memory_space=pltpu.VMEM)
ASPEC = pl.BlockSpec(memory_space=pl.ANY)
SSPEC = pl.BlockSpec(memory_space=pltpu.SMEM)


def lane_iota(shape):
    return lax.broadcasted_iota(jnp.int32, shape, len(shape) - 1)


def pin(values, space=pltpu.VMEM):
    return [pltpu.with_memory_space_constraint(item, space) for item in values]


def swap_pairs(count, first, periodic):
    pairs = []
    for low in range(first, count, 2):
        high = low + 1
        if high >= count:
            if not periodic:
                continue
            high -= count
        pairs += [(low, high), (high, low)]
    return pairs


EAST_HALO = 10


def own_columns(refs, rows):
    lane = lane_iota((rows[1], LANES))
    level, g = lane >> 4, lane & 15
    west = jnp.zeros((rows[1], LANES), f32)
    east = jnp.zeros((rows[1], LANES), f32)
    for l, (first, second) in enumerate(refs):
        mine = level == l
        west = jnp.where(mine, pltpu.roll(first[pl.ds(*rows), :], 16 * l + 2, 1), west)
        east = jnp.where(mine, pltpu.roll(second[pl.ds(*rows), :], (16 * l + 10) % LANES, 1), east)
    both = jnp.where((g >= 2) & (g < 6), west, jnp.where((g >= 6) & (g < EAST_HALO), east, 0.0))
    if len(refs) == 1:
        for shift in (16, 32, 64):
            both = both + pltpu.roll(both, shift, 1)
    return both


def join_strip(own, from_west, from_east, f):
    g = lane_iota(own.shape) & 15
    west = pltpu.roll(from_west, (-2 * f) % LANES, 1)
    east = pltpu.roll(from_east, (EAST_HALO - 2 * f) % LANES, 1)
    value = jnp.where(g < 2, west, own)
    return jnp.where((g >= EAST_HALO) & (g < EAST_HALO + 2), east, value)


def load_kernel(h_hbm, vel_hbm, bot_hbm, cor_hbm, red_hbm, h_ref, u_ref, v_ref, bc_ref, own_ref, a_ref, b_ref, red_ref, red, sem):
    levels, rows = h_hbm.shape[0], h_hbm.shape[1]
    copies = []
    for t in range(2):
        cols = pl.ds(t * LANES, LANES)
        body = pl.ds(PAD, rows)
        copies += [
            (h_hbm.at[:, :, cols], h_ref.at[:, t, body, :]),
            (vel_hbm.at[0, :, :, cols], u_ref.at[:, t, body, :]),
            (vel_hbm.at[1, :, :, cols], v_ref.at[:, t, body, :]),
            (bot_hbm.at[:, cols], bc_ref.at[0, t, body, :]),
            (cor_hbm.at[:, cols], bc_ref.at[1, t, body, :]),
        ]
    copies = [pltpu.make_async_copy(s, d, sem.at[i]) for i, (s, d) in enumerate(copies)]
    few = pltpu.make_async_copy(red_hbm, red, sem.at[10])
    for i in (0, 5, 1, 6, 2, 7, 3, 8, 4, 9):
        copies[i].start()
    few.start()
    gx = lax.axis_index("gx")
    even = gx % 2 == 0
    step = 32
    lane = lane_iota((step, LANES))

    for f in range(5):
        copies[f].wait()
        copies[5 + f].wait()
        if f == 1:
            @pl.when(gx == lax.axis_size("gx") - 1)
            def _():
                lane = lane_iota((rows, LANES))
                for l in range(levels):
                    edge = u_ref[l, 1, pl.ds(PAD, rows), :]
                    u_ref[l, 1, pl.ds(PAD, rows), :] = jnp.where(lane == LANES - 1, 0.0, edge)

        for k in range(rows // step):
            if f < 3:
                ref = (h_ref, u_ref, v_ref)[f]
                refs = [(ref.at[l, 0], ref.at[l, 1]) for l in range(levels)]
            else:
                refs = [(bc_ref.at[f - 3, 0], bc_ref.at[f - 3, 1])]
            own_ref[f, 0, pl.ds(PAD + k * step, step), :] = own_columns(refs, (PAD + k * step, step))
    for k in range(rows // step):
        west = jnp.zeros((step, LANES), f32)
        east = jnp.zeros((step, LANES), f32)
        for f in range(5):
            own = own_ref[f, 0, pl.ds(PAD + k * step, step), :]
            mine = ((lane & 15) >> 1) == f
            west = jnp.where(mine, pltpu.roll(own, (2 * f - 2) % LANES, 1), west)
            east = jnp.where(mine, pltpu.roll(own, (2 * f - 8) % LANES, 1), east)
        a_ref[pl.ds(k * step, step), :] = jnp.where(even, east, west)
        b_ref[pl.ds(k * step, step), :] = jnp.where(even, west, east)
    few.wait()
    for l in range(levels):
        red_ref[pl.ds(l, 1), :] = jnp.full((1, LANES), 2.0 * red[l], f32)


def rows_kernel(h_ref, u_ref, v_ref, bc_ref, north_ref, south_ref, own, bc):
    levels = h_ref.shape[0]
    rows = h_ref.shape[2] - 2 * PAD
    low, high = pl.ds(PAD, 6), pl.ds(PAD + rows - 6, 6)
    for src, dst in ((h_ref, own.at[0]), (u_ref, own.at[1]), (v_ref, own.at[2]), (bc_ref, bc)):
        for l in range(src.shape[0]):
            dst[l, :, pl.ds(PAD + 2, 6), :] = src[l, :, low, :]
            dst[l, :, pl.ds(PAD + 8, 6), :] = src[l, :, high, :]
    for t in range(2):
        cols = pl.ds(t * LANES, LANES)
        for f, ref in enumerate((h_ref, u_ref, v_ref)):
            for l in range(levels):
                spot = pl.ds(2 * (f * levels + l), 2)
                north_ref[spot, cols] = ref[l, t, pl.ds(PAD + rows - 2, 2), :]
                south_ref[spot, cols] = ref[l, t, pl.ds(PAD, 2), :]
        for f in range(2):
            spot = pl.ds(2 * (3 * levels + f), 2)
            north_ref[spot, cols] = bc_ref[f, t, pl.ds(PAD + rows - 2, 2), :]
            south_ref[spot, cols] = bc_ref[f, t, pl.ds(PAD, 2), :]


def corner_kernel(north_in, south_in, own_ref, ra, rb, after, north_ref, south_ref):
    rows = ra.shape[0]
    even = lax.axis_index("gx") % 2 == 0
    north_ref[0:MAIN, :] = north_in[0:MAIN, :]
    south_ref[0:MAIN, :] = south_in[0:MAIN, :]

    def tail(start, f):
        span = pl.ds(start, 8)
        r1, r2 = ra[span, :], rb[span, :]
        own = own_ref[f, 0, pl.ds(PAD + start, 8), :]
        return join_strip(own, jnp.where(even, r2, r1), jnp.where(even, r1, r2), f)

    for f in range(5):
        up, down = tail(rows - 8, f), tail(0, f)
        for r in range(2):
            cols = pl.ds(LANES * r, LANES)
            north_ref[pl.ds(MAIN + f, 1), cols] = up[6 + r : 7 + r, :]
            south_ref[pl.ds(MAIN + f, 1), cols] = down[r : r + 1, :]


def evaluate(fields, temps, height, spin, east, west, reduced, rows, step, update):
    h_ref, u_ref, v_ref = fields
    s_ref, fx_ref, fy_ref, b_ref, z_ref, vq_ref = temps

    def span(k, shift=0):
        return pl.ds(PAD + k * step + shift, step)

    def cells(k):
        h, hn = h_ref[:, span(k), :], h_ref[:, span(k, 1), :]
        u, un = u_ref[:, span(k), :], u_ref[:, span(k, 1), :]
        v, vs = v_ref[:, span(k), :], v_ref[:, span(k, -1), :]
        pair = h + east(h)
        square = u * u
        kinetic = 0.5 * (square + west(square) + v * v + vs * vs)
        s_ref[:, span(k), :] = pair
        fx_ref[:, span(k), :] = pair * u
        fy_ref[:, span(k), :] = (h + hn) * v
        b_ref[:, span(k), :] = kinetic + (height(k) + reduced * h)
        z_ref[:, span(k), :] = (east(v) - v) - (un - u) + spin(k)

    def finish(k):
        pair, pair_n = s_ref[:, span(k), :], s_ref[:, span(k, 1), :]
        fx, fxn = fx_ref[:, span(k), :], fx_ref[:, span(k, 1), :]
        fy, fys = fy_ref[:, span(k), :], fy_ref[:, span(k, -1), :]
        b, bn = b_ref[:, span(k), :], b_ref[:, span(k, 1), :]
        q = z_ref[:, span(k), :] / (pair + pair_n)
        uq = q * (fx + fxn)
        vq = q * (fy + east(fy))
        vq_ref[:, span(k), :] = vq
        dh = (fx - west(fx)) + (fy - fys)
        dv = (west(uq) + uq) + (bn - b)
        du = (vq_ref[:, span(k, -1), :] + vq) - (east(b) - b)
        update(k, dh, du, dv)

    count = rows // step
    cells(0)
    for k in range(count):
        if k + 1 < count:
            cells(k + 1)
        finish(k)


def span_of(k, step):
    return pl.ds(PAD + k * step, step)


def level_sum(values):
    for shift in (16, 32, 64):
        values = values + pltpu.roll(values, shift, values.ndim - 1)
    return values


def base(h_at, bc, height, rows, step):
    for k in range(rows // step):
        total = bc[0, :, span_of(k, step), :]
        for l in range(h_at.shape[0]):
            total = total + h_at[l, :, span_of(k, step), :]
        height[:, span_of(k, step), :] = total


def main_stage(now, temps, height, bc, reduced, rows, step, unroll, update, after=None):
    lane = lane_iota((1, step, LANES))

    def east(x):
        moved = pltpu.roll(x, LANES - 1, 2)
        return jnp.concatenate([jnp.where(lane == LANES - 1, moved[1:2], moved[0:1]), moved[1:2]], axis=0)

    def west(x):
        moved = pltpu.roll(x, 1, 2)
        return jnp.concatenate([moved[0:1], jnp.where(lane == 0, moved[0:1], moved[1:2])], axis=0)

    def one(l, slot):
        evaluate(
            [ref.at[l] for ref in now],
            [temps.at[slot, i] for i in range(6)],
            lambda k: height[:, span_of(k, step), :],
            lambda k: bc[1, :, span_of(k, step), :],
            east, west, reduced[pl.ds(l, 1), :][None], rows, step,
            lambda k, dh, du, dv: update(l, k, (dh, du, dv)),
        )
        if after is not None:
            after(l)

    levels = now[0].shape[0]

    def some(j, carry):
        for slot in range(unroll):
            one(j * unroll + slot, slot)
        return carry

    if unroll == levels:
        some(0, 0)
    else:
        lax.fori_loop(0, levels // unroll, some, 0)


def strip_stages(strips, mid, acc, temps, reduced, gx, size_x, rows, step):
    lane = lane_iota((1, step, LANES))
    g = lane & 15
    west_out = (g < 2) & (gx == 0)
    out = west_out | ((g >= EAST_HALO) & (gx == size_x - 1))
    out_u = west_out | ((g >= EAST_HALO - 1) & (gx == size_x - 1))
    small = lane_iota((1, 1, LANES))
    red_lane = jnp.zeros((1, 1, LANES), f32)
    for l in range(8):
        red_lane = jnp.where((small >> 4) == l, reduced[l : l + 1, :][None], red_lane)

    def stage(now, update):
        def height(k):
            return strips[3, :, span_of(k, step), :] + level_sum(now[0, :, span_of(k, step), :])

        evaluate(
            [now.at[i] for i in range(3)],
            [temps.at[i] for i in range(6)],
            height,
            lambda k: strips[4, :, span_of(k, step), :],
            lambda x: pltpu.roll(x, LANES - 1, 2),
            lambda x: pltpu.roll(x, 1, 2),
            red_lane, rows, step, update,
        )

    def first(k, *rates):
        for i, rate in enumerate(rates):
            start = strips[i, :, span_of(k, step), :]
            mid[i, :, span_of(k, step), :] = jnp.where(out_u if i == 1 else out, 0.0, start + RATE[i] * time_step * rate)
            acc[i, :, span_of(k, step), :] = start + RATE[i] * half_step * rate

    def second(k, *rates):
        for i, rate in enumerate(rates):
            value = acc[i, :, span_of(k, step), :] + RATE[i] * half_step * rate
            value = jnp.where(out_u, 0.0, value) if i == 1 else value
            acc[i, :, span_of(k, step), :] = jnp.where(g < 2, pltpu.roll(value, LANES - 8, 2), value)

    stage(strips, first)
    stage(mid, second)


def first_update(fields, mid, acc, step):
    def update(l, k, rates):
        for i, rate in enumerate(rates):
            start = fields[i][l, :, span_of(k, step), :]
            mid[i, l, :, span_of(k, step), :] = start + RATE[i] * time_step * rate
            acc[i, l, :, pl.ds(k * step, step), :] = start + RATE[i] * half_step * rate

    return update


def second_update(acc, strip, step, emit):
    lane = lane_iota((step, LANES))

    def update(l, k, rates):
        for i, rate in enumerate(rates):
            value = acc[i, l, :, pl.ds(k * step, step), :] + RATE[i] * half_step * rate
            edge = pltpu.roll(strip[i, 0, span_of(k, step), :], LANES - 2 - 16 * l, 1)
            emit(i, l, k, jnp.where(lane < 2, edge, value[0]), jnp.where(lane >= LANES - 2, edge, value[1]))

    return update


def first_kernel(h_ref, u_ref, v_ref, bc_ref, reduced, mid, acc, height, temps):
    rows = h_ref.shape[2] - 2 * PAD
    step = 8
    base(h_ref, bc_ref, height, rows, step)
    main_stage((h_ref, u_ref, v_ref), temps, height, bc_ref, reduced, rows, step, UNROLL,
               first_update((h_ref, u_ref, v_ref), mid, acc, step))


def second_body(own_ref, ra, rb, mid, acc, bc_ref, reduced, h_out, vel_out, edge_ref, strip_ref,
                result, sem, strip_mid, strip_acc, height, temps, strip_temps):
    gx, size_x = lax.axis_index("gx"), lax.axis_size("gx")
    rows = ra.shape[0]
    even_x = gx % 2 == 0
    r1, r2 = ra[...], rb[...]
    from_west, from_east = jnp.where(even_x, r2, r1), jnp.where(even_x, r1, r2)
    for f in range(5):
        strip_ref[f, 0, pl.ds(PAD, rows), :] = join_strip(own_ref[f, 0, pl.ds(PAD, rows), :], from_west, from_east, f)
    step = 8
    last = rows // step - 1
    strip_stages(strip_ref, strip_mid, strip_acc, strip_temps, reduced, gx, size_x, rows, 16)
    base(mid.at[0], bc_ref, height, rows, step)

    def emit(i, l, k, *tiles):
        for t, value in enumerate(tiles):
            if k == 0 or k == last:
                edge_ref[i, l, t, pl.ds(0 if k == 0 else step, step), :] = value
            else:
                result[i, l, t, pl.ds(k * step, step), :] = value

    body = pl.ds(step, rows - 2 * step)
    levels = mid.shape[1]

    def copies(l):
        out = []
        for t in range(2):
            cols = pl.ds(t * LANES, LANES)
            for i, target in enumerate((h_out.at[l], vel_out.at[0, l], vel_out.at[1, l])):
                source = result.at[i, l, t, body, :]
                out.append(pltpu.make_async_copy(source, target.at[body, cols], sem.at[l, 3 * t + i]))
        return out

    main_stage([mid.at[i] for i in range(3)], temps, height, bc_ref, reduced, rows, step, UNROLL,
               second_update(acc, strip_acc, step, emit), lambda l: [copy.start() for copy in copies(l)])

    def finish(l, carry):
        for copy in copies(l):
            copy.wait()
        return carry

    lax.fori_loop(0, levels, finish, 0)


def store(result, h_out, vel_out, sem, spans):
    copies = []
    for t in range(2):
        cols = pl.ds(t * LANES, LANES)
        for src, dst in spans:
            copies += [
                (result.at[0, :, t, src, :], h_out.at[:, dst, cols]),
                (result.at[1, :, t, src, :], vel_out.at[0, :, dst, cols]),
                (result.at[2, :, t, src, :], vel_out.at[1, :, dst, cols]),
            ]
    copies = [pltpu.make_async_copy(s, d, sem.at[i]) for i, (s, d) in enumerate(copies)]
    for copy in copies:
        copy.start()
    for copy in copies:
        copy.wait()


def early_kernel(own_ref, ra, rb, mid, acc, bc_ref, reduced, y_in, h_out, vel_out, edge_ref, strip_ref, y_out, *work):
    @pl.when(lax.axis_index("gy") == 0)
    def _():
        second_body(own_ref, ra, rb, mid, acc, bc_ref, reduced, h_out, vel_out, edge_ref, strip_ref, *work)


def late_kernel(own_ref, ra, rb, mid, acc, bc_ref, reduced, h_in, vel_in, edge_in, strip_in,
                h_out, vel_out, edge_ref, strip_ref, *work):
    @pl.when(lax.axis_index("gy") != 0)
    def _():
        second_body(own_ref, ra, rb, mid, acc, bc_ref, reduced, h_out, vel_out, edge_ref, strip_ref, *work)


def outer_kernel(strip_ref, m0, m1, reduced, own_in, bc_in, edge_in, h_in, vel_in,
                 h_out, vel_out, own, bc, result, strips, mid, acc, sem, strip_mid, strip_acc, height, temps, strip_temps):
    gx, size_x = lax.axis_index("gx"), lax.axis_size("gx")
    levels = own.shape[1]
    rows = h_out.shape[1]
    top, bottom = PAD, PAD + 8
    low, high = pl.ds(PAD, 6), pl.ds(PAD + rows - 6, 6)

    south, north = m0[...], m1[...]

    for t in range(2):
        cols = slice(t * LANES, (t + 1) * LANES)

        def place(dst, index, spot):
            dst[(*index, t, pl.ds(top, 2), slice(None))] = south[spot : spot + 2, cols]
            dst[(*index, t, pl.ds(bottom + 6, 2), slice(None))] = north[spot : spot + 2, cols]

        for f in range(3):
            for l in range(levels):
                place(own, (f, l), 2 * (f * levels + l))
        for f in range(2):
            place(bc, (f,), 2 * (3 * levels + f))
    for f in range(5):
        for r in range(2):
            cols = slice(r * LANES, (r + 1) * LANES)
            strips[f, 0, pl.ds(top + r, 1), :] = south[MAIN + f : MAIN + f + 1, cols]
            strips[f, 0, pl.ds(bottom + 6 + r, 1), :] = north[MAIN + f : MAIN + f + 1, cols]
        strips[f, 0, pl.ds(top + 2, 6), :] = strip_ref[f, 0, low, :]
        strips[f, 0, pl.ds(bottom, 6), :] = strip_ref[f, 0, high, :]

    strip_stages(strips, strip_mid, strip_acc, strip_temps, reduced, gx, size_x, 16, 16)
    fields = [own.at[i] for i in range(3)]
    base(fields[0], bc, height, 16, 16)
    main_stage(fields, temps, height, bc, reduced, 16, 16, levels, first_update(fields, mid, acc, 16))
    base(mid.at[0], bc, height, 16, 16)
    def emit(i, l, k, *tiles):
        for t, value in enumerate(tiles):
            result[i, l, t, pl.ds(0, 2), :] = value[2:4, :]
            result[i, l, t, pl.ds(14, 2), :] = value[12:14, :]

    main_stage([mid.at[i] for i in range(3)], temps, height, bc, reduced, 16, 16, levels,
               second_update(acc, strip_acc, 16, emit))
    store(result, h_out, vel_out, sem, ((pl.ds(0, 8), pl.ds(0, 8)), (pl.ds(8, 8), pl.ds(rows - 8, 8))))


def work_shapes(rows, unroll):
    total = rows + 2 * PAD
    return [
        VM((3, 1, total, LANES), f32),
        VM((3, 1, total, LANES), f32),
        VM((2, total, LANES), f32),
        VM((unroll, 6, 2, total, LANES), f32),
        VM((6, 1, total, LANES), f32),
    ]


def body(thickness, velocity, bottom, coriolis, reduced):
    levels, rows, columns = thickness.shape
    total = rows + 2 * PAD
    field = VM((levels, 2, total, LANES), f32)
    strip = VM((5, 1, total, LANES), f32)
    message_x, message_y = VM((rows, LANES), f32), VM((64, 2 * LANES), f32)
    h_shape = jax.ShapeDtypeStruct(thickness.shape, f32)
    vel_shape = jax.ShapeDtypeStruct(velocity.shape, f32)
    edge_shape = VM((3, levels, 2, 16, LANES), f32)

    def call(kernel, name, out_shape, in_specs, args, out_specs=None, scratch=(), limit=SMALL, aliases={}):
        return pl.pallas_call(
            kernel,
            out_shape=out_shape,
            in_specs=in_specs,
            out_specs=out_specs or [VSPEC] * len(out_shape),
            scratch_shapes=list(scratch),
            input_output_aliases=aliases,
            compiler_params=pltpu.CompilerParams(vmem_limit_bytes=limit),
            name=name,
        )(*args)

    size_x, size_y = lax.axis_size("gx"), lax.axis_size("gy")

    args = pin((thickness, velocity, bottom, coriolis, reduced), pltpu.HBM)
    h, u, v, bc, own, sa, sb, red = pin(call(
        load_kernel, "load",
        [field, field, field, VM((2, 2, total, LANES), f32), strip, message_x, message_x, VM((levels, LANES), f32)],
        [ASPEC] * 5, args, scratch=[pltpu.SMEM((levels,), f32), pltpu.SemaphoreType.DMA((11,))],
    ))
    ra, rb = pin([lax.ppermute(item, "gx", swap_pairs(size_x, i, False)) for i, item in enumerate((sa, sb))])
    edge_fields, edge_fixed = VM((3, levels, 2, 32, LANES), f32), VM((2, 2, 32, LANES), f32)
    north, south, own_edge, bc_edge = pin(call(
        rows_kernel, "edges", [message_y] * 2 + [edge_fields, edge_fixed], [VSPEC] * 4, (h, u, v, bc),
    ))
    mid, acc = pin(call(
        first_kernel, "first",
        [VM((3, levels, 2, total, LANES), f32), VM((3, levels, 2, rows, LANES), f32)],
        [VSPEC] * 5, (h, u, v, bc, red),
        scratch=[VM((2, total, LANES), f32), VM((UNROLL, 6, 2, total, LANES), f32)],
    ))
    y0, y1 = pin(call(
        corner_kernel, "corners", [message_y] * 2, [VSPEC] * 6, (north, south, own, ra, rb, mid),
    ))
    m0, = pin([lax.ppermute(y0, "gy", [(i, (i + 1) % size_y) for i in range(size_y)])])
    work = [VM((3, levels, 2, rows, LANES), f32), pltpu.SemaphoreType.DMA((levels, 6)), *work_shapes(rows, UNROLL)]
    outs = [h_shape, vel_shape, edge_shape, strip]
    specs = [ASPEC, ASPEC, VSPEC, VSPEC]
    h_new, vel_new, edge, strips, y1 = call(
        early_kernel, "early", outs + [message_y], [VSPEC] * 8,
        (own, ra, rb, mid, acc, bc, red, y1), specs + [VSPEC], work, LARGE, {7: 4},
    )
    y1, edge, strips = pin([y1, edge, strips])
    (m1,) = pin([lax.ppermute(y1, "gy", [(i, (i - 1) % size_y) for i in range(size_y)])])
    h_new, vel_new, edge, strips = call(
        late_kernel, "late", outs, [VSPEC] * 7 + [ASPEC, ASPEC, VSPEC, VSPEC],
        (own, ra, rb, mid, acc, bc, red, h_new, vel_new, edge, strips), specs, work, LARGE,
        {7: 0, 8: 1, 9: 2, 10: 3},
    )
    edge, strips = pin([edge, strips])
    return tuple(call(
        outer_kernel, "outer", [h_shape, vel_shape, edge_fields, edge_fixed, edge_shape],
        [VSPEC] * 7 + [ASPEC, ASPEC],
        (strips, m0, m1, red, own_edge, bc_edge, edge, h_new, vel_new),
        [ASPEC, ASPEC, VSPEC, VSPEC, VSPEC],
        [
            VM((5, 1, 32, LANES), f32),
            VM((3, levels, 2, 32, LANES), f32),
            VM((3, levels, 2, 16, LANES), f32),
            pltpu.SemaphoreType.DMA((12,)),
            *work_shapes(16, levels),
        ],
        LARGE, {7: 0, 8: 1, 4: 2, 5: 3, 6: 4},
    )[:2])


def solution(mesh):
    return jax.shard_map(
        body,
        mesh=mesh,
        in_specs=(
            P(None, "gy", "gx"),
            P(None, None, "gy", "gx"),
            P("gy", "gx"),
            P("gy", "gx"),
            P(),
        ),
        out_specs=(P(None, "gy", "gx"), P(None, None, "gy", "gx")),
        check_vma=False,
    )
```

```python
import jax
import jax.numpy as jnp
from jax import lax
from jax.experimental import pallas as pl
from jax.experimental.pallas import tpu as pltpu
from jax.sharding import PartitionSpec as P


time_step = 0.1
half_step = 0.05
PAD = 8
LANES = 128
SMALL, LARGE = 4 << 20, 16 << 20
MAIN = 52
CHUNK = 64
ORDER = (3, 4, 0, 1, 2)
EARLY = (7, 5)
RATE = (-0.5, 0.5, -0.5)
f32 = jnp.float32
VM = pltpu.VMEM
VSPEC = pl.BlockSpec(memory_space=pltpu.VMEM)
ASPEC = pl.BlockSpec(memory_space=pl.ANY)
SSPEC = pl.BlockSpec(memory_space=pltpu.SMEM)


def lane_iota(shape):
    return lax.broadcasted_iota(jnp.int32, shape, len(shape) - 1)


def pin(values, space=pltpu.VMEM):
    return [pltpu.with_memory_space_constraint(item, space) for item in values]


def swap_pairs(count, first, periodic):
    pairs = []
    for low in range(first, count, 2):
        high = low + 1
        if high >= count:
            if not periodic:
                continue
            high -= count
        pairs += [(low, high), (high, low)]
    return pairs


EAST_HALO = 10


def own_columns(refs, rows):
    lane = lane_iota((rows[1], LANES))
    level, g = lane >> 4, lane & 15
    index = jnp.where(g < 6, jnp.maximum(g - 2, 0), jnp.minimum(g + (LANES - EAST_HALO), LANES - 1))
    both = jnp.zeros((rows[1], LANES), f32)
    for l, (first, second) in enumerate(refs):
        ends = jnp.where(lane < LANES // 2, first[pl.ds(*rows), :], second[pl.ds(*rows), :])
        moved = jnp.take_along_axis(ends, index, axis=1, mode="promise_in_bounds")
        both = moved if len(refs) == 1 else jnp.where(level == l, moved, both)
    return jnp.where((g >= 2) & (g < EAST_HALO), both, 0.0)


def join_strip(own, from_west, from_east, f):
    g = lane_iota(own.shape) & 15
    west = pltpu.roll(from_west, (-2 * f) % LANES, 1)
    east = pltpu.roll(from_east, (EAST_HALO - 2 * f) % LANES, 1)
    value = jnp.where(g < 2, west, own)
    return jnp.where((g >= EAST_HALO) & (g < EAST_HALO + 2), east, value)


def load_kernel(h_hbm, vel_hbm, bot_hbm, cor_hbm, red_hbm, h_ref, uv_ref, bc_ref, own_ref, a_ref, b_ref, red_ref,
                red, sem):
    levels, rows = h_hbm.shape[0], h_hbm.shape[1]
    body = pl.ds(PAD, rows)
    copies = []
    for t in range(2):
        cols = pl.ds(t * LANES, LANES)
        copies += [
            (h_hbm.at[:, :, cols], h_ref.at[:, t, body, :]),
            (vel_hbm.at[0, :, :, cols], uv_ref.at[0, :, t, body, :]),
            (vel_hbm.at[1, :, :, cols], uv_ref.at[1, :, t, body, :]),
            (bot_hbm.at[:, cols], bc_ref.at[0, t, body, :]),
            (cor_hbm.at[:, cols], bc_ref.at[1, t, body, :]),
        ]
    copies = [pltpu.make_async_copy(s, d, sem.at[i]) for i, (s, d) in enumerate(copies)]
    few = pltpu.make_async_copy(red_hbm, red, sem.at[10])
    for i in ORDER:
        copies[i].start()
        copies[5 + i].start()
    few.start()
    gx = lax.axis_index("gx")
    even = gx % 2 == 0
    step = CHUNK
    lane = lane_iota((step, LANES))
    wall = ((lane & 15) == EAST_HALO - 1) & (gx == lax.axis_size("gx") - 1)
    for f in ORDER:
        copies[f].wait()
        copies[5 + f].wait()
        if f < 3:
            ref = (h_ref, uv_ref.at[0], uv_ref.at[1])[f]
            refs = [(ref.at[l, 0], ref.at[l, 1]) for l in range(levels)]
        else:
            refs = [(bc_ref.at[f - 3, 0], bc_ref.at[f - 3, 1])]
        mine = ((lane & 15) >> 1) == f

        def chunk(k):
            start = k * step
            own = own_columns(refs, (start + PAD, step))
            if f == 1:
                own = jnp.where(wall, 0.0, own)
            own_ref[f, 0, pl.ds(start + PAD, step), :] = own
            west = pltpu.roll(own, (2 * f - 2) % LANES, 1)
            east = pltpu.roll(own, (2 * f - 8) % LANES, 1)
            for ref, value in ((a_ref, jnp.where(even, east, west)), (b_ref, jnp.where(even, west, east))):
                span = pl.ds(start, step)
                ref[span, :] = jnp.where(mine, value, 0.0 if f == ORDER[0] else ref[span, :])

        for k in range(rows // step):
            chunk(k)
    few.wait()
    for l in range(levels):
        red_ref[pl.ds(l, 1), :] = jnp.full((1, LANES), 2.0 * red[l], f32)


def rows_kernel(h_ref, bc_ref, uv_in, uv_ref, north_ref, south_ref, own, bc):
    levels = h_ref.shape[0]
    rows = h_ref.shape[2] - 2 * PAD
    u_ref, v_ref = uv_ref.at[0], uv_ref.at[1]

    @pl.when(lax.axis_index("gx") == lax.axis_size("gx") - 1)
    def _():
        lane = lane_iota((rows, LANES))
        for l in range(levels):
            edge = u_ref[l, 1, pl.ds(PAD, rows), :]
            u_ref[l, 1, pl.ds(PAD, rows), :] = jnp.where(lane == LANES - 1, 0.0, edge)

    low, high = pl.ds(PAD, 6), pl.ds(PAD + rows - 6, 6)
    for src, dst in ((h_ref, own.at[0]), (u_ref, own.at[1]), (v_ref, own.at[2]), (bc_ref, bc)):
        for l in range(src.shape[0]):
            dst[l, :, pl.ds(PAD + 2, 6), :] = src[l, :, low, :]
            dst[l, :, pl.ds(PAD + 8, 6), :] = src[l, :, high, :]
    for t in range(2):
        cols = pl.ds(t * LANES, LANES)
        for f, ref in enumerate((h_ref, u_ref, v_ref)):
            for l in range(levels):
                spot = pl.ds(2 * (f * levels + l), 2)
                north_ref[spot, cols] = ref[l, t, pl.ds(PAD + rows - 2, 2), :]
                south_ref[spot, cols] = ref[l, t, pl.ds(PAD, 2), :]
        for f in range(2):
            spot = pl.ds(2 * (3 * levels + f), 2)
            north_ref[spot, cols] = bc_ref[f, t, pl.ds(PAD + rows - 2, 2), :]
            south_ref[spot, cols] = bc_ref[f, t, pl.ds(PAD, 2), :]


def corner_kernel(north_in, south_in, own_ref, ra, rb, after, north_ref, south_ref):
    rows = ra.shape[0]
    even = lax.axis_index("gx") % 2 == 0
    north_ref[0:MAIN, :] = north_in[0:MAIN, :]
    south_ref[0:MAIN, :] = south_in[0:MAIN, :]

    def tail(start, f):
        span = pl.ds(start, 8)
        r1, r2 = ra[span, :], rb[span, :]
        own = own_ref[f, 0, pl.ds(PAD + start, 8), :]
        return join_strip(own, jnp.where(even, r2, r1), jnp.where(even, r1, r2), f)

    for f in range(5):
        up, down = tail(rows - 8, f), tail(0, f)
        for r in range(2):
            cols = pl.ds(LANES * r, LANES)
            north_ref[pl.ds(MAIN + f, 1), cols] = up[6 + r : 7 + r, :]
            south_ref[pl.ds(MAIN + f, 1), cols] = down[r : r + 1, :]


def evaluate(fields, temps, height, spin, east, west, reduced, rows, step, update):
    h_ref, u_ref, v_ref = fields
    s_ref, fx_ref, fy_ref, b_ref, z_ref, vq_ref = temps

    def span(k, shift=0):
        return pl.ds(PAD + k * step + shift, step)

    def cells(k):
        h, hn = h_ref[:, span(k), :], h_ref[:, span(k, 1), :]
        u, un = u_ref[:, span(k), :], u_ref[:, span(k, 1), :]
        v, vs = v_ref[:, span(k), :], v_ref[:, span(k, -1), :]
        pair = h + east(h)
        square = u * u
        kinetic = 0.5 * (square + west(square) + v * v + vs * vs)
        s_ref[:, span(k), :] = pair
        fx_ref[:, span(k), :] = pair * u
        fy_ref[:, span(k), :] = (h + hn) * v
        b_ref[:, span(k), :] = kinetic + (height(k) + reduced * h)
        z_ref[:, span(k), :] = (east(v) - v) - (un - u) + spin(k)

    def finish(k):
        pair, pair_n = s_ref[:, span(k), :], s_ref[:, span(k, 1), :]
        fx, fxn = fx_ref[:, span(k), :], fx_ref[:, span(k, 1), :]
        fy, fys = fy_ref[:, span(k), :], fy_ref[:, span(k, -1), :]
        b, bn = b_ref[:, span(k), :], b_ref[:, span(k, 1), :]
        q = z_ref[:, span(k), :] / (pair + pair_n)
        uq = q * (fx + fxn)
        vq = q * (fy + east(fy))
        vq_ref[:, span(k), :] = vq
        dh = (fx - west(fx)) + (fy - fys)
        dv = (west(uq) + uq) + (bn - b)
        du = (vq_ref[:, span(k, -1), :] + vq) - (east(b) - b)
        update(k, dh, du, dv)

    count = rows // step
    cells(0)
    for k in range(count):
        if k + 1 < count:
            cells(k + 1)
        finish(k)


def span_of(k, step):
    return pl.ds(PAD + k * step, step)


def level_sum(values):
    for shift in (16, 32, 64):
        values = values + pltpu.roll(values, shift, values.ndim - 1)
    return values


def base(h_at, bc, height, rows, step):
    for k in range(rows // step):
        total = bc[0, :, span_of(k, step), :]
        for l in range(h_at.shape[0]):
            total = total + h_at[l, :, span_of(k, step), :]
        height[:, span_of(k, step), :] = total


def main_stage(now, temps, height, bc, reduced, rows, step, unroll, update, after=None, low=0, high=None):
    lane = lane_iota((1, step, LANES))

    def east(x):
        moved = pltpu.roll(x, LANES - 1, 2)
        return jnp.concatenate([jnp.where(lane == LANES - 1, moved[1:2], moved[0:1]), moved[1:2]], axis=0)

    def west(x):
        moved = pltpu.roll(x, 1, 2)
        return jnp.concatenate([moved[0:1], jnp.where(lane == 0, moved[0:1], moved[1:2])], axis=0)

    def one(l, slot):
        evaluate(
            [ref.at[l] for ref in now],
            [temps.at[slot, i] for i in range(6)],
            lambda k: height[:, span_of(k, step), :],
            lambda k: bc[1, :, span_of(k, step), :],
            east, west, reduced[pl.ds(l, 1), :][None], rows, step,
            lambda k, dh, du, dv: update(l, k, (dh, du, dv)),
        )
        if after is not None:
            after(l)

    def single(l, carry):
        one(l, 0)
        return carry

    high = now[0].shape[0] if high is None else high
    if unroll == 1:
        lax.fori_loop(low, high, single, 0)
    else:
        for l in range(unroll):
            one(l, l)


def strip_stages(strips, mid, acc, temps, reduced, gx, size_x, rows, step):
    lane = lane_iota((1, step, LANES))
    g = lane & 15
    west_out = (g < 2) & (gx == 0)
    out = west_out | ((g >= EAST_HALO) & (gx == size_x - 1))
    out_u = west_out | ((g >= EAST_HALO - 1) & (gx == size_x - 1))
    small = lane_iota((1, 1, LANES))
    red_lane = jnp.zeros((1, 1, LANES), f32)
    for l in range(8):
        red_lane = jnp.where((small >> 4) == l, reduced[l : l + 1, :][None], red_lane)

    def stage(now, update):
        def height(k):
            return strips[3, :, span_of(k, step), :] + level_sum(now[0, :, span_of(k, step), :])

        evaluate(
            [now.at[i] for i in range(3)],
            [temps.at[i] for i in range(6)],
            height,
            lambda k: strips[4, :, span_of(k, step), :],
            lambda x: pltpu.roll(x, LANES - 1, 2),
            lambda x: pltpu.roll(x, 1, 2),
            red_lane, rows, step, update,
        )

    def first(k, *rates):
        for i, rate in enumerate(rates):
            start = strips[i, :, span_of(k, step), :]
            mid[i, :, span_of(k, step), :] = jnp.where(out_u if i == 1 else out, 0.0, start + RATE[i] * time_step * rate)
            acc[i, :, span_of(k, step), :] = start + RATE[i] * half_step * rate

    def second(k, *rates):
        for i, rate in enumerate(rates):
            value = acc[i, :, span_of(k, step), :] + RATE[i] * half_step * rate
            value = jnp.where(out_u, 0.0, value) if i == 1 else value
            acc[i, :, span_of(k, step), :] = jnp.where(g < 2, pltpu.roll(value, LANES - 8, 2), value)

    stage(strips, first)
    stage(mid, second)


def first_update(fields, mid, acc, step):
    def update(l, k, rates):
        for i, rate in enumerate(rates):
            start = fields[i][l, :, span_of(k, step), :]
            mid[i, l, :, span_of(k, step), :] = start + RATE[i] * time_step * rate
            acc[i, l, :, pl.ds(k * step, step), :] = start + RATE[i] * half_step * rate

    return update


def second_update(acc, strip, step, emit):
    lane = lane_iota((step, LANES))

    def update(l, k, rates):
        for i, rate in enumerate(rates):
            value = acc[i, l, :, pl.ds(k * step, step), :] + RATE[i] * half_step * rate
            edge = pltpu.roll(strip[i, 0, span_of(k, step), :], LANES - 2 - 16 * l, 1)
            emit(i, l, k, jnp.where(lane < 2, edge, value[0]), jnp.where(lane >= LANES - 2, edge, value[1]))

    return update


def first_kernel(h_ref, uv_ref, bc_ref, reduced, mid, acc, height, temps):
    fields = (h_ref, uv_ref.at[0], uv_ref.at[1])
    rows = h_ref.shape[2] - 2 * PAD
    step = 8
    base(h_ref, bc_ref, height, rows, step)
    main_stage(fields, temps, height, bc_ref, reduced, rows, step, 1, first_update(fields, mid, acc, step))


def prepare(own_ref, ra, rb, mid, bc_ref, reduced, strip_ref, strip_acc, height, strip_mid, strip_temps):
    gx, size_x = lax.axis_index("gx"), lax.axis_size("gx")
    rows = ra.shape[0]
    even_x = gx % 2 == 0
    r1, r2 = ra[...], rb[...]
    from_west, from_east = jnp.where(even_x, r2, r1), jnp.where(even_x, r1, r2)
    for f in range(5):
        strip_ref[f, 0, pl.ds(PAD, rows), :] = join_strip(own_ref[f, 0, pl.ds(PAD, rows), :], from_west, from_east, f)
    strip_stages(strip_ref, strip_mid, strip_acc, strip_temps, reduced, gx, size_x, rows, 16)
    base(mid.at[0], bc_ref, height, rows, 8)


def second_levels(low, high, mid, acc, bc_ref, reduced, h_out, vel_out, edge_ref, strip_acc, height, result, sem, temps):
    rows = acc.shape[3]
    step = 8
    last = rows // step - 1
    body = pl.ds(step, rows - 2 * step)

    def emit(i, l, k, *tiles):
        for t, value in enumerate(tiles):
            if k == 0 or k == last:
                edge_ref[i, l, pl.ds(0 if k == 0 else step, step), pl.ds(t * LANES, LANES)] = value
            else:
                result[i, l, pl.ds(k * step, step), pl.ds(t * LANES, LANES)] = value

    def copies(l):
        targets = (h_out.at[l], vel_out.at[0, l], vel_out.at[1, l])
        return [
            pltpu.make_async_copy(result.at[i, l, body, :], target.at[body, :], sem.at[l, i])
            for i, target in enumerate(targets)
        ]

    main_stage([mid.at[i] for i in range(3)], temps, height, bc_ref, reduced, rows, step, 1,
               second_update(acc, strip_acc, step, emit), lambda l: [copy.start() for copy in copies(l)], low, high)

    def finish(l, carry):
        for copy in copies(l):
            copy.wait()
        return carry

    lax.fori_loop(low, high, finish, 0)


def store(result, h_out, vel_out, sem, spans):
    copies = []
    for src, dst in spans:
        copies += [
            (result.at[0, :, src, :], h_out.at[:, dst, :]),
            (result.at[1, :, src, :], vel_out.at[0, :, dst, :]),
            (result.at[2, :, src, :], vel_out.at[1, :, dst, :]),
        ]
    copies = [pltpu.make_async_copy(s, d, sem.at[i]) for i, (s, d) in enumerate(copies)]
    for copy in copies:
        copy.start()
    for copy in copies:
        copy.wait()


def early_count(levels):
    return jnp.clip(EARLY[0] - lax.axis_index("gy") * EARLY[1] // 2, 0, levels)


def early_kernel(own_ref, ra, rb, mid, acc, bc_ref, reduced, y_in, h_out, vel_out, edge_ref, strip_ref, strip_acc, height,
                 y_out, result, sem, strip_mid, temps, strip_temps):
    count = early_count(mid.shape[1])

    @pl.when(count > 0)
    def _():
        prepare(own_ref, ra, rb, mid, bc_ref, reduced, strip_ref, strip_acc, height, strip_mid, strip_temps)
        second_levels(0, count, mid, acc, bc_ref, reduced, h_out, vel_out, edge_ref, strip_acc, height, result, sem, temps)


def late_kernel(own_ref, ra, rb, mid, acc, bc_ref, reduced, h_in, vel_in, edge_in, strip_in, strip_acc_in, height_in,
                h_out, vel_out, edge_ref, strip_ref, strip_acc, height, result, sem, strip_mid, temps, strip_temps):
    levels = mid.shape[1]
    count = early_count(levels)

    @pl.when(count == 0)
    def _():
        prepare(own_ref, ra, rb, mid, bc_ref, reduced, strip_ref, strip_acc, height, strip_mid, strip_temps)

    @pl.when(count < levels)
    def _():
        second_levels(count, levels, mid, acc, bc_ref, reduced, h_out, vel_out, edge_ref, strip_acc, height, result, sem, temps)


def outer_kernel(strip_ref, m0, m1, reduced, own_in, bc_in, edge_in, h_in, vel_in,
                 h_out, vel_out, own, bc, result, strips, mid, acc, small_bc, sem, strip_mid, strip_acc, strip_end, height,
                 temps, strip_temps):
    gx, size_x = lax.axis_index("gx"), lax.axis_size("gx")
    levels = own.shape[1]
    rows = h_out.shape[1]
    top, bottom = PAD, PAD + 8
    low, high = pl.ds(PAD, 6), pl.ds(PAD + rows - 6, 6)

    south, north = m0[...], m1[...]

    for t in range(2):
        cols = slice(t * LANES, (t + 1) * LANES)

        def place(dst, index, spot):
            dst[(*index, t, pl.ds(top, 2), slice(None))] = south[spot : spot + 2, cols]
            dst[(*index, t, pl.ds(bottom + 6, 2), slice(None))] = north[spot : spot + 2, cols]

        for f in range(3):
            for l in range(levels):
                place(own, (f, l), 2 * (f * levels + l))
        for f in range(2):
            place(bc, (f,), 2 * (3 * levels + f))
    for f in range(5):
        for r in range(2):
            cols = slice(r * LANES, (r + 1) * LANES)
            strips[f, 0, pl.ds(top + r, 1), :] = south[MAIN + f : MAIN + f + 1, cols]
            strips[f, 0, pl.ds(bottom + 6 + r, 1), :] = north[MAIN + f : MAIN + f + 1, cols]
        strips[f, 0, pl.ds(top + 2, 6), :] = strip_ref[f, 0, low, :]
        strips[f, 0, pl.ds(bottom, 6), :] = strip_ref[f, 0, high, :]

    strip_stages(strips, strip_mid, strip_acc, strip_temps, reduced, gx, size_x, 16, 16)
    halves = ((pl.ds(PAD, 4), slice(1, 5)), (pl.ds(PAD + 4, 4), slice(11, 15)))
    for dst, src in halves:
        for i in range(3):
            strip_end[i, 0, dst, :] = strip_acc[i, 0, pl.ds(PAD + src.start, 4), :]
        for f in range(2):
            small_bc[f, :, dst, :] = bc[f, :, pl.ds(PAD + src.start, 4), :]
    fields = [own.at[i] for i in range(3)]
    base(fields[0], bc, height, 16, 16)

    def first(l, k, rates):
        for i, rate in enumerate(rates):
            start = fields[i][l, :, span_of(0, 16), :]
            middle, total = start + RATE[i] * time_step * rate, start + RATE[i] * half_step * rate
            for dst, src in halves:
                mid[i, l, :, dst, :] = middle[:, src, :]
                acc[i, l, :, pl.ds(dst.start - PAD, 4), :] = total[:, src, :]

    main_stage(fields, temps, height, bc, reduced, 16, 16, levels, first)
    base(mid.at[0], small_bc, height, 8, 8)

    def emit(i, l, k, *tiles):
        for t, value in enumerate(tiles):
            cols = pl.ds(t * LANES, LANES)
            result[i, l, pl.ds(0, 2), cols] = value[1:3, :]
            result[i, l, pl.ds(14, 2), cols] = value[5:7, :]

    main_stage([mid.at[i] for i in range(3)], temps, height, small_bc, reduced, 8, 8, levels,
               second_update(acc, strip_end, 8, emit))
    store(result, h_out, vel_out, sem, ((pl.ds(0, 8), pl.ds(0, 8)), (pl.ds(8, 8), pl.ds(rows - 8, 8))))


def body(thickness, velocity, bottom, coriolis, reduced):
    levels, rows, columns = thickness.shape
    total = rows + 2 * PAD
    field = VM((levels, 2, total, LANES), f32)
    strip = VM((5, 1, total, LANES), f32)
    message_x, message_y = VM((rows, LANES), f32), VM((64, 2 * LANES), f32)
    h_shape = jax.ShapeDtypeStruct(thickness.shape, f32)
    vel_shape = jax.ShapeDtypeStruct(velocity.shape, f32)
    edge_shape = VM((3, levels, 16, 2 * LANES), f32)

    def call(kernel, name, out_shape, in_specs, args, out_specs=None, scratch=(), limit=SMALL, aliases={}):
        return pl.pallas_call(
            kernel,
            out_shape=out_shape,
            in_specs=in_specs,
            out_specs=out_specs or [VSPEC] * len(out_shape),
            scratch_shapes=list(scratch),
            input_output_aliases=aliases,
            compiler_params=pltpu.CompilerParams(vmem_limit_bytes=limit),
            name=name,
        )(*args)

    size_x, size_y = lax.axis_size("gx"), lax.axis_size("gy")

    args = pin((thickness, velocity, bottom, coriolis, reduced), pltpu.HBM)
    uv_shape = VM((2, levels, 2, total, LANES), f32)
    h, uv, bc, own, sa, sb, red = pin(call(
        load_kernel, "load",
        [field, uv_shape, VM((2, 2, total, LANES), f32), strip, message_x, message_x, VM((levels, LANES), f32)],
        [ASPEC] * 5, args,
        scratch=[
            pltpu.SMEM((levels,), f32),
            pltpu.SemaphoreType.DMA((11,)),
        ],
    ))
    ra, rb = pin([lax.ppermute(item, "gx", swap_pairs(size_x, i, False)) for i, item in enumerate((sa, sb))])
    edge_fields, edge_fixed = VM((3, levels, 2, 32, LANES), f32), VM((2, 2, 32, LANES), f32)
    uv, north, south, own_edge, bc_edge = pin(call(
        rows_kernel, "edges", [uv_shape] + [message_y] * 2 + [edge_fields, edge_fixed], [VSPEC] * 3, (h, bc, uv),
        aliases={2: 0},
    ))
    temps = VM((1, 6, 2, total, LANES), f32)
    strip_temps = VM((6, 1, total, LANES), f32)
    strip_part, height = VM((3, 1, total, LANES), f32), VM((2, total, LANES), f32)
    mid, acc = pin(call(
        first_kernel, "first",
        [VM((3, levels, 2, total, LANES), f32), VM((3, levels, 2, rows, LANES), f32)],
        [VSPEC] * 4, (h, uv, bc, red), scratch=[height, temps],
    ))
    y0, y1 = pin(call(
        corner_kernel, "corners", [message_y] * 2, [VSPEC] * 6, (north, south, own, ra, rb, mid),
    ))
    (m0,) = pin([lax.ppermute(y0, "gy", [(i, (i + 1) % size_y) for i in range(size_y)])])
    work = [VM((3, levels, rows, 2 * LANES), f32), pltpu.SemaphoreType.DMA((levels, 3)), strip_part, temps, strip_temps]
    outs = [h_shape, vel_shape, edge_shape, strip, strip_part, height]
    specs = [ASPEC, ASPEC] + [VSPEC] * 4
    h_new, vel_new, *kept, y1 = call(
        early_kernel, "early", outs + [message_y], [VSPEC] * 8,
        (own, ra, rb, mid, acc, bc, red, y1), specs + [VSPEC], work, LARGE, {7: 6},
    )
    *kept, y1 = pin([*kept, y1])
    (m1,) = pin([lax.ppermute(y1, "gy", [(i, (i - 1) % size_y) for i in range(size_y)])])
    h_new, vel_new, edge, strips, *_ = call(
        late_kernel, "late", outs, [VSPEC] * 7 + [ASPEC, ASPEC] + [VSPEC] * 4,
        (own, ra, rb, mid, acc, bc, red, h_new, vel_new, *kept), specs, work, LARGE,
        {7 + i: i for i in range(6)},
    )
    edge, strips = pin([edge, strips])
    part = VM((3, 1, 32, LANES), f32)
    return tuple(call(
        outer_kernel, "outer", [h_shape, vel_shape, edge_fields, edge_fixed, edge_shape],
        [VSPEC] * 7 + [ASPEC, ASPEC],
        (strips, m0, m1, red, own_edge, bc_edge, edge, h_new, vel_new),
        [ASPEC, ASPEC, VSPEC, VSPEC, VSPEC],
        [
            VM((5, 1, 32, LANES), f32),
            VM((3, levels, 2, 24, LANES), f32),
            VM((3, levels, 2, 8, LANES), f32),
            VM((2, 2, 24, LANES), f32),
            pltpu.SemaphoreType.DMA((6,)),
            part,
            part,
            part,
            VM((2, 32, LANES), f32),
            VM((levels, 6, 2, 32, LANES), f32),
            VM((6, 1, 32, LANES), f32),
        ],
        LARGE, {7: 0, 8: 1, 4: 2, 5: 3, 6: 4},
    )[:2])


def solution(mesh):
    return jax.shard_map(
        body,
        mesh=mesh,
        in_specs=(
            P(None, "gy", "gx"),
            P(None, None, "gy", "gx"),
            P("gy", "gx"),
            P("gy", "gx"),
            P(),
        ),
        out_specs=(P(None, "gy", "gx"), P(None, None, "gy", "gx")),
        check_vma=False,
    )
```

```python
import jax
import jax.numpy as jnp
from jax import lax
from jax.experimental import pallas as pl
from jax.experimental.pallas import tpu as pltpu
from jax.sharding import PartitionSpec as P


time_step = 0.1
half_step = 0.05
PAD = 8
LANES = 128
SMALL, LARGE = 4 << 20, 16 << 20
MAIN = 52
CHUNK = 64
ORDER = (3, 4, 0, 1, 2)
EARLY = (7, 5)
RATE = (-0.5, 0.5, -0.5)
f32 = jnp.float32
VM = pltpu.VMEM
VSPEC = pl.BlockSpec(memory_space=pltpu.VMEM)
ASPEC = pl.BlockSpec(memory_space=pl.ANY)
SSPEC = pl.BlockSpec(memory_space=pltpu.SMEM)


def lane_iota(shape):
    return lax.broadcasted_iota(jnp.int32, shape, len(shape) - 1)


def pin(values, space=pltpu.VMEM):
    return [pltpu.with_memory_space_constraint(item, space) for item in values]


def swap_pairs(count, first, periodic):
    pairs = []
    for low in range(first, count, 2):
        high = low + 1
        if high >= count:
            if not periodic:
                continue
            high -= count
        pairs += [(low, high), (high, low)]
    return pairs


EAST_HALO = 10


def own_columns(refs, rows):
    lane = lane_iota((rows[1], LANES))
    level, g = lane >> 4, lane & 15
    index = jnp.where(g < 6, jnp.maximum(g - 2, 0), jnp.minimum(g + (LANES - EAST_HALO), LANES - 1))
    both = jnp.zeros((rows[1], LANES), f32)
    for l, (first, second) in enumerate(refs):
        ends = jnp.where(lane < LANES // 2, first[pl.ds(*rows), :], second[pl.ds(*rows), :])
        moved = jnp.take_along_axis(ends, index, axis=1, mode="promise_in_bounds")
        both = moved if len(refs) == 1 else jnp.where(level == l, moved, both)
    return jnp.where((g >= 2) & (g < EAST_HALO), both, 0.0)


def join_strip(own, from_west, from_east, f):
    g = lane_iota(own.shape) & 15
    west = pltpu.roll(from_west, (-2 * f) % LANES, 1)
    east = pltpu.roll(from_east, (EAST_HALO - 2 * f) % LANES, 1)
    value = jnp.where(g < 2, west, own)
    return jnp.where((g >= EAST_HALO) & (g < EAST_HALO + 2), east, value)


def load_kernel(h_hbm, vel_hbm, bot_hbm, cor_hbm, red_hbm, h_ref, uv_ref, bc_ref, own_ref, a_ref, b_ref, red_ref,
                red, sem):
    levels, rows = h_hbm.shape[0], h_hbm.shape[1]
    body = pl.ds(PAD, rows)
    copies = []
    for t in range(2):
        cols = pl.ds(t * LANES, LANES)
        copies += [
            (h_hbm.at[:, :, cols], h_ref.at[:, t, body, :]),
            (vel_hbm.at[0, :, :, cols], uv_ref.at[0, :, t, body, :]),
            (vel_hbm.at[1, :, :, cols], uv_ref.at[1, :, t, body, :]),
            (bot_hbm.at[:, cols], bc_ref.at[0, t, body, :]),
            (cor_hbm.at[:, cols], bc_ref.at[1, t, body, :]),
        ]
    copies = [pltpu.make_async_copy(s, d, sem.at[i]) for i, (s, d) in enumerate(copies)]
    few = pltpu.make_async_copy(red_hbm, red, sem.at[10])
    for i in ORDER:
        copies[i].start()
        copies[5 + i].start()
    few.start()
    gx = lax.axis_index("gx")
    even = gx % 2 == 0
    step = CHUNK
    lane = lane_iota((step, LANES))
    wall = ((lane & 15) == EAST_HALO - 1) & (gx == lax.axis_size("gx") - 1)
    for f in ORDER:
        copies[f].wait()
        copies[5 + f].wait()
        if f < 3:
            ref = (h_ref, uv_ref.at[0], uv_ref.at[1])[f]
            refs = [(ref.at[l, 0], ref.at[l, 1]) for l in range(levels)]
        else:
            refs = [(bc_ref.at[f - 3, 0], bc_ref.at[f - 3, 1])]
        mine = ((lane & 15) >> 1) == f

        def chunk(k):
            start = k * step
            own = own_columns(refs, (start + PAD, step))
            if f == 1:
                own = jnp.where(wall, 0.0, own)
            own_ref[f, 0, pl.ds(start + PAD, step), :] = own
            west = pltpu.roll(own, (2 * f - 2) % LANES, 1)
            east = pltpu.roll(own, (2 * f - 8) % LANES, 1)
            for ref, value in ((a_ref, jnp.where(even, east, west)), (b_ref, jnp.where(even, west, east))):
                span = pl.ds(start, step)
                ref[span, :] = jnp.where(mine, value, 0.0 if f == ORDER[0] else ref[span, :])

        for k in range(rows // step):
            chunk(k)
    few.wait()
    for l in range(levels):
        red_ref[pl.ds(l, 1), :] = jnp.full((1, LANES), 2.0 * red[l], f32)


def rows_kernel(h_ref, bc_ref, uv_in, uv_ref, north_ref, south_ref, own, bc, late_bc):
    levels = h_ref.shape[0]
    rows = h_ref.shape[2] - 2 * PAD
    u_ref, v_ref = uv_ref.at[0], uv_ref.at[1]

    @pl.when(lax.axis_index("gx") == lax.axis_size("gx") - 1)
    def _():
        lane = lane_iota((rows, LANES))
        for l in range(levels):
            edge = u_ref[l, 1, pl.ds(PAD, rows), :]
            u_ref[l, 1, pl.ds(PAD, rows), :] = jnp.where(lane == LANES - 1, 0.0, edge)

    low, high = pl.ds(PAD, 2), pl.ds(PAD + rows - 2, 2)
    for src, dst in ((h_ref, own.at[0]), (u_ref, own.at[1]), (v_ref, own.at[2]), (bc_ref, bc)):
        for l in range(src.shape[0]):
            dst[l, :, pl.ds(PAD + 2, 2), :] = src[l, :, low, :]
            dst[l, :, pl.ds(PAD + 4, 2), :] = src[l, :, high, :]
    for f in range(2):
        late_bc[f, :, pl.ds(PAD + 1, 3), :] = bc_ref[f, :, pl.ds(PAD, 3), :]
        late_bc[f, :, pl.ds(PAD + 4, 3), :] = bc_ref[f, :, pl.ds(PAD + rows - 3, 3), :]
    for t in range(2):
        cols = pl.ds(t * LANES, LANES)
        for f, ref in enumerate((h_ref, u_ref, v_ref)):
            for l in range(levels):
                spot = pl.ds(2 * (f * levels + l), 2)
                north_ref[spot, cols] = ref[l, t, pl.ds(PAD + rows - 2, 2), :]
                south_ref[spot, cols] = ref[l, t, pl.ds(PAD, 2), :]
        for f in range(2):
            spot = pl.ds(2 * (3 * levels + f), 2)
            north_ref[spot, cols] = bc_ref[f, t, pl.ds(PAD + rows - 2, 2), :]
            south_ref[spot, cols] = bc_ref[f, t, pl.ds(PAD, 2), :]


def corner_kernel(north_in, south_in, own_ref, ra, rb, after, north_ref, south_ref):
    rows = ra.shape[0]
    even = lax.axis_index("gx") % 2 == 0
    north_ref[0:MAIN, :] = north_in[0:MAIN, :]
    south_ref[0:MAIN, :] = south_in[0:MAIN, :]

    def tail(start, f):
        span = pl.ds(start, 8)
        r1, r2 = ra[span, :], rb[span, :]
        own = own_ref[f, 0, pl.ds(PAD + start, 8), :]
        return join_strip(own, jnp.where(even, r2, r1), jnp.where(even, r1, r2), f)

    for f in range(5):
        up, down = tail(rows - 8, f), tail(0, f)
        for r in range(2):
            cols = pl.ds(LANES * r, LANES)
            north_ref[pl.ds(MAIN + f, 1), cols] = up[6 + r : 7 + r, :]
            south_ref[pl.ds(MAIN + f, 1), cols] = down[r : r + 1, :]


def evaluate(fields, temps, height, spin, east, west, reduced, rows, step, update):
    h_ref, u_ref, v_ref = fields
    s_ref, fx_ref, fy_ref, b_ref, z_ref, vq_ref = temps

    def span(k, shift=0):
        return pl.ds(PAD + k * step + shift, step)

    def cells(k):
        h, hn = h_ref[:, span(k), :], h_ref[:, span(k, 1), :]
        u, un = u_ref[:, span(k), :], u_ref[:, span(k, 1), :]
        v, vs = v_ref[:, span(k), :], v_ref[:, span(k, -1), :]
        pair = h + east(h)
        square = u * u
        kinetic = 0.5 * (square + west(square) + v * v + vs * vs)
        s_ref[:, span(k), :] = pair
        fx_ref[:, span(k), :] = pair * u
        fy_ref[:, span(k), :] = (h + hn) * v
        b_ref[:, span(k), :] = kinetic + (height(k) + reduced * h)
        z_ref[:, span(k), :] = (east(v) - v) - (un - u) + spin(k)

    def finish(k):
        pair, pair_n = s_ref[:, span(k), :], s_ref[:, span(k, 1), :]
        fx, fxn = fx_ref[:, span(k), :], fx_ref[:, span(k, 1), :]
        fy, fys = fy_ref[:, span(k), :], fy_ref[:, span(k, -1), :]
        b, bn = b_ref[:, span(k), :], b_ref[:, span(k, 1), :]
        q = z_ref[:, span(k), :] / (pair + pair_n)
        uq = q * (fx + fxn)
        vq = q * (fy + east(fy))
        vq_ref[:, span(k), :] = vq
        dh = (fx - west(fx)) + (fy - fys)
        dv = (west(uq) + uq) + (bn - b)
        du = (vq_ref[:, span(k, -1), :] + vq) - (east(b) - b)
        update(k, dh, du, dv)

    count = rows // step
    cells(0)
    for k in range(count):
        if k + 1 < count:
            cells(k + 1)
        finish(k)


def span_of(k, step):
    return pl.ds(PAD + k * step, step)


def level_sum(values):
    for shift in (16, 32, 64):
        values = values + pltpu.roll(values, shift, values.ndim - 1)
    return values


def base(h_at, bc, height, rows, step):
    for k in range(rows // step):
        total = bc[0, :, span_of(k, step), :]
        for l in range(h_at.shape[0]):
            total = total + h_at[l, :, span_of(k, step), :]
        height[:, span_of(k, step), :] = total


def main_stage(now, temps, height, bc, reduced, rows, step, unroll, update, after=None, low=0, high=None):
    lane = lane_iota((1, step, LANES))

    def east(x):
        moved = pltpu.roll(x, LANES - 1, 2)
        return jnp.concatenate([jnp.where(lane == LANES - 1, moved[1:2], moved[0:1]), moved[1:2]], axis=0)

    def west(x):
        moved = pltpu.roll(x, 1, 2)
        return jnp.concatenate([moved[0:1], jnp.where(lane == 0, moved[0:1], moved[1:2])], axis=0)

    def one(l, slot):
        evaluate(
            [ref.at[l] for ref in now],
            [temps.at[slot, i] for i in range(6)],
            lambda k: height[:, span_of(k, step), :],
            lambda k: bc[1, :, span_of(k, step), :],
            east, west, reduced[pl.ds(l, 1), :][None], rows, step,
            lambda k, dh, du, dv: update(l, k, (dh, du, dv)),
        )
        if after is not None:
            after(l)

    def single(l, carry):
        one(l, 0)
        return carry

    high = now[0].shape[0] if high is None else high
    if unroll == 1:
        lax.fori_loop(low, high, single, 0)
    else:
        for l in range(unroll):
            one(l, l)


def strip_masks(reduced, gx, size_x, step):
    g = lane_iota((1, step, LANES)) & 15
    west_out = (g < 2) & (gx == 0)
    out = west_out | ((g >= EAST_HALO) & (gx == size_x - 1))
    out_u = west_out | ((g >= EAST_HALO - 1) & (gx == size_x - 1))
    small = lane_iota((1, 1, LANES))
    red_lane = jnp.zeros((1, 1, LANES), f32)
    for l in range(8):
        red_lane = jnp.where((small >> 4) == l, reduced[l : l + 1, :][None], red_lane)
    return (out, out_u, out), red_lane


def strip_stage(now, strips, temps, red_lane, rows, step, update):
    evaluate(
        [now.at[i] for i in range(3)],
        [temps.at[i] for i in range(6)],
        lambda k: strips[3, :, span_of(k, step), :] + level_sum(now[0, :, span_of(k, step), :]),
        lambda k: strips[4, :, span_of(k, step), :],
        lambda x: pltpu.roll(x, LANES - 1, 2),
        lambda x: pltpu.roll(x, 1, 2),
        red_lane, rows, step, update,
    )


def strip_last(acc, out_u, step):
    g = lane_iota((1, step, LANES)) & 15

    def update(k, *rates):
        for i, rate in enumerate(rates):
            value = acc[i, :, span_of(k, step), :] + RATE[i] * half_step * rate
            value = jnp.where(out_u, 0.0, value) if i == 1 else value
            acc[i, :, span_of(k, step), :] = jnp.where(g < 2, pltpu.roll(value, LANES - 8, 2), value)

    return update


def strip_stages(strips, mid, acc, temps, reduced, gx, size_x, rows, step):
    masks, red_lane = strip_masks(reduced, gx, size_x, step)

    def first(k, *rates):
        for i, rate in enumerate(rates):
            start = strips[i, :, span_of(k, step), :]
            mid[i, :, span_of(k, step), :] = jnp.where(masks[i], 0.0, start + RATE[i] * time_step * rate)
            acc[i, :, span_of(k, step), :] = start + RATE[i] * half_step * rate

    strip_stage(strips, strips, temps, red_lane, rows, step, first)
    strip_stage(mid, strips, temps, red_lane, rows, step, strip_last(acc, masks[1], step))


def first_update(fields, mid, acc, late_mid, late_acc, step, last):
    def update(l, k, rates):
        for i, rate in enumerate(rates):
            start = fields[i][l, :, span_of(k, step), :]
            middle, total = start + RATE[i] * time_step * rate, start + RATE[i] * half_step * rate
            mid[i, l, :, span_of(k, step), :] = middle
            acc[i, l, :, pl.ds(k * step, step), :] = total
            if k == 0:
                late_mid[i, l, :, pl.ds(PAD + 2, 2), :] = middle[:, 1:3, :]
                late_acc[i, l, :, pl.ds(2, 1), :] = total[:, 1:2, :]
            if k == last:
                late_mid[i, l, :, pl.ds(PAD + 4, 2), :] = middle[:, step - 3 : step - 1, :]
                late_acc[i, l, :, pl.ds(5, 1), :] = total[:, step - 2 : step - 1, :]

    return update


def second_update(acc, strip, step, emit):
    lane = lane_iota((step, LANES))

    def update(l, k, rates):
        for i, rate in enumerate(rates):
            value = acc[i, l, :, pl.ds(k * step, step), :] + RATE[i] * half_step * rate
            edge = pltpu.roll(strip[i, 0, span_of(k, step), :], LANES - 2 - 16 * l, 1)
            emit(i, l, k, jnp.where(lane < 2, edge, value[0]), jnp.where(lane >= LANES - 2, edge, value[1]))

    return update


def first_kernel(h_ref, uv_ref, bc_ref, reduced, mid, acc, late_mid, late_acc, height, temps):
    fields = (h_ref, uv_ref.at[0], uv_ref.at[1])
    rows = h_ref.shape[2] - 2 * PAD
    step = 8
    base(h_ref, bc_ref, height, rows, step)
    main_stage(fields, temps, height, bc_ref, reduced, rows, step, 1,
               first_update(fields, mid, acc, late_mid, late_acc, step, rows // step - 1))


def prepare(own_ref, ra, rb, mid, bc_ref, reduced, strip_ref, strip_acc, height, strip_mid, strip_temps):
    gx, size_x = lax.axis_index("gx"), lax.axis_size("gx")
    rows = ra.shape[0]
    even_x = gx % 2 == 0
    r1, r2 = ra[...], rb[...]
    from_west, from_east = jnp.where(even_x, r2, r1), jnp.where(even_x, r1, r2)
    for f in range(5):
        strip_ref[f, 0, pl.ds(PAD, rows), :] = join_strip(own_ref[f, 0, pl.ds(PAD, rows), :], from_west, from_east, f)
    strip_stages(strip_ref, strip_mid, strip_acc, strip_temps, reduced, gx, size_x, rows, 16)
    base(mid.at[0], bc_ref, height, rows, 8)


def second_levels(low, high, mid, acc, bc_ref, reduced, h_out, vel_out, edge_ref, strip_acc, height, result, sem, temps):
    rows = acc.shape[3]
    step = 8
    last = rows // step - 1
    body = pl.ds(step, rows - 2 * step)

    def emit(i, l, k, *tiles):
        for t, value in enumerate(tiles):
            if k == 0 or k == last:
                edge_ref[i, l, pl.ds(0 if k == 0 else step, step), pl.ds(t * LANES, LANES)] = value
            else:
                result[i, l, pl.ds(k * step, step), pl.ds(t * LANES, LANES)] = value

    def copies(l):
        targets = (h_out.at[l], vel_out.at[0, l], vel_out.at[1, l])
        return [
            pltpu.make_async_copy(result.at[i, l, body, :], target.at[body, :], sem.at[l, i])
            for i, target in enumerate(targets)
        ]

    main_stage([mid.at[i] for i in range(3)], temps, height, bc_ref, reduced, rows, step, 1,
               second_update(acc, strip_acc, step, emit), lambda l: [copy.start() for copy in copies(l)], low, high)

    def finish(l, carry):
        for copy in copies(l):
            copy.wait()
        return carry

    lax.fori_loop(low, high, finish, 0)


def store(result, h_out, vel_out, sem, spans):
    copies = []
    for src, dst in spans:
        copies += [
            (result.at[0, :, src, :], h_out.at[:, dst, :]),
            (result.at[1, :, src, :], vel_out.at[0, :, dst, :]),
            (result.at[2, :, src, :], vel_out.at[1, :, dst, :]),
        ]
    copies = [pltpu.make_async_copy(s, d, sem.at[i]) for i, (s, d) in enumerate(copies)]
    for copy in copies:
        copy.start()
    for copy in copies:
        copy.wait()


def early_count(levels):
    return jnp.clip(EARLY[0] - lax.axis_index("gy") * EARLY[1] // 2, 0, levels)


def early_kernel(own_ref, ra, rb, mid, acc, bc_ref, reduced, y_in, h_out, vel_out, edge_ref, strip_ref, strip_acc, height,
                 strip_mid, y_out, result, sem, temps, strip_temps):
    count = early_count(mid.shape[1])

    @pl.when(count > 0)
    def _():
        prepare(own_ref, ra, rb, mid, bc_ref, reduced, strip_ref, strip_acc, height, strip_mid, strip_temps)
        second_levels(0, count, mid, acc, bc_ref, reduced, h_out, vel_out, edge_ref, strip_acc, height, result, sem, temps)


def late_kernel(own_ref, ra, rb, mid, acc, bc_ref, reduced, h_in, vel_in, edge_in, strip_in, strip_acc_in, height_in,
                strip_mid_in, h_out, vel_out, edge_ref, strip_ref, strip_acc, height, strip_mid, result, sem, temps, strip_temps):
    levels = mid.shape[1]
    count = early_count(levels)

    @pl.when(count == 0)
    def _():
        prepare(own_ref, ra, rb, mid, bc_ref, reduced, strip_ref, strip_acc, height, strip_mid, strip_temps)

    @pl.when(count < levels)
    def _():
        second_levels(count, levels, mid, acc, bc_ref, reduced, h_out, vel_out, edge_ref, strip_acc, height, result, sem, temps)


def outer_kernel(strip_ref, strip_mid_ref, m0, m1, reduced, own_in, bc_in, late_bc_in, mid_in, acc_in, edge_in, h_in, vel_in,
                 h_out, vel_out, own, bc, late_bc, mid, acc, result, strips, late_strips, sem, strip_mid, strip_acc, height,
                 temps, strip_temps):
    gx, size_x = lax.axis_index("gx"), lax.axis_size("gx")
    levels = own.shape[1]
    rows = h_out.shape[1]
    south, north = m0[...], m1[...]

    for t in range(2):
        cols = slice(t * LANES, (t + 1) * LANES)

        def place(dst, index, spot):
            dst[(*index, t, pl.ds(PAD, 2), slice(None))] = south[spot : spot + 2, cols]
            dst[(*index, t, pl.ds(PAD + 6, 2), slice(None))] = north[spot : spot + 2, cols]

        for f in range(3):
            for l in range(levels):
                place(own, (f, l), 2 * (f * levels + l))
        for f in range(2):
            spot = 2 * (3 * levels + f)
            place(bc, (f,), spot)
            late_bc[f, t, pl.ds(PAD, 1), :] = south[spot + 1 : spot + 2, cols]
            late_bc[f, t, pl.ds(PAD + 7, 1), :] = north[spot : spot + 1, cols]
    for f in range(5):
        before, after = south[MAIN + f : MAIN + f + 1, :], north[MAIN + f : MAIN + f + 1, :]
        strips[f, 0, pl.ds(PAD, 1), :] = before[:, :LANES]
        strips[f, 0, pl.ds(PAD + 1, 1), :] = before[:, LANES:]
        strips[f, 0, pl.ds(PAD + 2, 2), :] = strip_ref[f, 0, pl.ds(PAD, 2), :]
        strips[f, 0, pl.ds(PAD + 4, 2), :] = strip_ref[f, 0, pl.ds(PAD + rows - 2, 2), :]
        strips[f, 0, pl.ds(PAD + 6, 1), :] = after[:, :LANES]
        strips[f, 0, pl.ds(PAD + 7, 1), :] = after[:, LANES:]
        if f >= 3:
            late_strips[f, 0, pl.ds(PAD, 1), :] = before[:, LANES:]
            late_strips[f, 0, pl.ds(PAD + 1, 3), :] = strip_ref[f, 0, pl.ds(PAD, 3), :]
            late_strips[f, 0, pl.ds(PAD + 4, 3), :] = strip_ref[f, 0, pl.ds(PAD + rows - 3, 3), :]
            late_strips[f, 0, pl.ds(PAD + 7, 1), :] = after[:, :LANES]
    for i in range(3):
        for src, dst, kept in ((1, 2, 1), (rows - 3, 4, rows - 2)):
            strip_mid[i, 0, pl.ds(PAD + dst, 2), :] = strip_mid_ref[i, 0, pl.ds(PAD + src, 2), :]
            start, middle = strip_ref[i, 0, pl.ds(PAD + kept, 1), :], strip_mid_ref[i, 0, pl.ds(PAD + kept, 1), :]
            strip_acc[i, 0, pl.ds(PAD + (2 if kept == 1 else 5), 1), :] = 0.5 * (start + middle)

    masks, red_lane = strip_masks(reduced, gx, size_x, 8)

    def strip_first(k, *rates):
        for i, rate in enumerate(rates):
            start = strips[i, :, span_of(0, 8), :]
            middle = jnp.where(masks[i], 0.0, start + RATE[i] * time_step * rate)
            total = start + RATE[i] * half_step * rate
            strip_mid[i, :, pl.ds(PAD, 2), :] = middle[:, 1:3, :]
            strip_mid[i, :, pl.ds(PAD + 6, 2), :] = middle[:, 5:7, :]
            strip_acc[i, :, pl.ds(PAD + 1, 1), :] = total[:, 2:3, :]
            strip_acc[i, :, pl.ds(PAD + 6, 1), :] = total[:, 5:6, :]

    strip_stage(strips, strips, strip_temps, red_lane, 8, 8, strip_first)
    strip_stage(strip_mid, late_strips, strip_temps, red_lane, 8, 8, strip_last(strip_acc, masks[1], 8))

    fields = [own.at[i] for i in range(3)]
    base(fields[0], bc, height, 8, 8)

    def first(l, k, rates):
        for i, rate in enumerate(rates):
            start = fields[i][l, :, span_of(0, 8), :]
            middle, total = start + RATE[i] * time_step * rate, start + RATE[i] * half_step * rate
            mid[i, l, :, pl.ds(PAD, 2), :] = middle[:, 1:3, :]
            mid[i, l, :, pl.ds(PAD + 6, 2), :] = middle[:, 5:7, :]
            acc[i, l, :, pl.ds(1, 1), :] = total[:, 2:3, :]
            acc[i, l, :, pl.ds(6, 1), :] = total[:, 5:6, :]

    main_stage(fields, temps, height, bc, reduced, 8, 8, levels, first)
    base(mid.at[0], late_bc, height, 8, 8)

    def emit(i, l, k, *tiles):
        for t, value in enumerate(tiles):
            cols = pl.ds(t * LANES, LANES)
            result[i, l, pl.ds(0, 2), cols] = value[1:3, :]
            result[i, l, pl.ds(14, 2), cols] = value[5:7, :]

    main_stage([mid.at[i] for i in range(3)], temps, height, late_bc, reduced, 8, 8, levels,
               second_update(acc, strip_acc, 8, emit))
    store(result, h_out, vel_out, sem, ((pl.ds(0, 8), pl.ds(0, 8)), (pl.ds(8, 8), pl.ds(rows - 8, 8))))


def body(thickness, velocity, bottom, coriolis, reduced):
    levels, rows, columns = thickness.shape
    total = rows + 2 * PAD
    field = VM((levels, 2, total, LANES), f32)
    strip = VM((5, 1, total, LANES), f32)
    message_x, message_y = VM((rows, LANES), f32), VM((64, 2 * LANES), f32)
    h_shape = jax.ShapeDtypeStruct(thickness.shape, f32)
    vel_shape = jax.ShapeDtypeStruct(velocity.shape, f32)
    edge_shape = VM((3, levels, 16, 2 * LANES), f32)

    def call(kernel, name, out_shape, in_specs, args, out_specs=None, scratch=(), limit=SMALL, aliases={}):
        return pl.pallas_call(
            kernel,
            out_shape=out_shape,
            in_specs=in_specs,
            out_specs=out_specs or [VSPEC] * len(out_shape),
            scratch_shapes=list(scratch),
            input_output_aliases=aliases,
            compiler_params=pltpu.CompilerParams(vmem_limit_bytes=limit),
            name=name,
        )(*args)

    size_x, size_y = lax.axis_size("gx"), lax.axis_size("gy")

    args = pin((thickness, velocity, bottom, coriolis, reduced), pltpu.HBM)
    uv_shape = VM((2, levels, 2, total, LANES), f32)
    h, uv, bc, own, sa, sb, red = pin(call(
        load_kernel, "load",
        [field, uv_shape, VM((2, 2, total, LANES), f32), strip, message_x, message_x, VM((levels, LANES), f32)],
        [ASPEC] * 5, args,
        scratch=[
            pltpu.SMEM((levels,), f32),
            pltpu.SemaphoreType.DMA((11,)),
        ],
    ))
    ra, rb = pin([lax.ppermute(item, "gx", swap_pairs(size_x, i, False)) for i, item in enumerate((sa, sb))])
    edge_fields, edge_fixed = VM((3, levels, 2, 24, LANES), f32), VM((2, 2, 24, LANES), f32)
    edge_sums = VM((3, levels, 2, 8, LANES), f32)
    uv, north, south, own_edge, bc_edge, late_bc = pin(call(
        rows_kernel, "edges", [uv_shape] + [message_y] * 2 + [edge_fields, edge_fixed, edge_fixed], [VSPEC] * 3, (h, bc, uv),
        aliases={2: 0},
    ))
    temps = VM((1, 6, 2, total, LANES), f32)
    strip_temps = VM((6, 1, total, LANES), f32)
    strip_part, height = VM((3, 1, total, LANES), f32), VM((2, total, LANES), f32)
    mid, acc, late_mid, late_acc = pin(call(
        first_kernel, "first",
        [VM((3, levels, 2, total, LANES), f32), VM((3, levels, 2, rows, LANES), f32), edge_fields, edge_sums],
        [VSPEC] * 4, (h, uv, bc, red), scratch=[height, temps],
    ))
    y0, y1 = pin(call(
        corner_kernel, "corners", [message_y] * 2, [VSPEC] * 6, (north, south, own, ra, rb, mid),
    ))
    (m0,) = pin([lax.ppermute(y0, "gy", [(i, (i + 1) % size_y) for i in range(size_y)])])
    work = [VM((3, levels, rows, 2 * LANES), f32), pltpu.SemaphoreType.DMA((levels, 3)), temps, strip_temps]
    outs = [h_shape, vel_shape, edge_shape, strip, strip_part, height, strip_part]
    specs = [ASPEC, ASPEC] + [VSPEC] * 5
    h_new, vel_new, *kept, y1 = call(
        early_kernel, "early", outs + [message_y], [VSPEC] * 8,
        (own, ra, rb, mid, acc, bc, red, y1), specs + [VSPEC], work, LARGE, {7: 7},
    )
    *kept, y1 = pin([*kept, y1])
    (m1,) = pin([lax.ppermute(y1, "gy", [(i, (i - 1) % size_y) for i in range(size_y)])])
    h_new, vel_new, edge, strips, _, _, strip_mid = call(
        late_kernel, "late", outs, [VSPEC] * 7 + [ASPEC, ASPEC] + [VSPEC] * 5,
        (own, ra, rb, mid, acc, bc, red, h_new, vel_new, *kept), specs, work, LARGE,
        {7 + i: i for i in range(7)},
    )
    edge, strips, strip_mid = pin([edge, strips, strip_mid])
    part = VM((3, 1, 24, LANES), f32)
    strip_small = VM((5, 1, 24, LANES), f32)
    return tuple(call(
        outer_kernel, "outer",
        [h_shape, vel_shape, edge_fields, edge_fixed, edge_fixed, edge_fields, edge_sums, edge_shape],
        [VSPEC] * 11 + [ASPEC, ASPEC],
        (strips, strip_mid, m0, m1, red, own_edge, bc_edge, late_bc, late_mid, late_acc, edge, h_new, vel_new),
        [ASPEC, ASPEC] + [VSPEC] * 6,
        [
            strip_small,
            strip_small,
            pltpu.SemaphoreType.DMA((6,)),
            part,
            part,
            VM((2, 24, LANES), f32),
            VM((levels, 6, 2, 24, LANES), f32),
            VM((6, 1, 24, LANES), f32),
        ],
        LARGE, {11: 0, 12: 1, 5: 2, 6: 3, 7: 4, 8: 5, 9: 6, 10: 7},
    )[:2])


def solution(mesh):
    return jax.shard_map(
        body,
        mesh=mesh,
        in_specs=(
            P(None, "gy", "gx"),
            P(None, None, "gy", "gx"),
            P("gy", "gx"),
            P("gy", "gx"),
            P(),
        ),
        out_specs=(P(None, "gy", "gx"), P(None, None, "gy", "gx")),
        check_vma=False,
    )
```

```python
import jax
import jax.numpy as jnp
from jax import lax
from jax.experimental import pallas as pl
from jax.experimental.pallas import tpu as pltpu
from jax.sharding import PartitionSpec as P


time_step = 0.1
half_step = 0.05
PAD = 8
LANES = 128
SMALL, LARGE = 4 << 20, 16 << 20
MAIN = 52
STRIP_ROWS = ((52, 52), (53, 53), (54, 54), (55, 55), (48, 51))
CHUNK = 64
ORDER = (3, 4, 0, 1, 2)
EARLY = (6, 4)
RATE = (-0.5, 0.5, -0.5)
f32 = jnp.float32
VM = pltpu.VMEM
VSPEC = pl.BlockSpec(memory_space=pltpu.VMEM)
ASPEC = pl.BlockSpec(memory_space=pl.ANY)
SSPEC = pl.BlockSpec(memory_space=pltpu.SMEM)


def lane_iota(shape):
    return lax.broadcasted_iota(jnp.int32, shape, len(shape) - 1)


def pin(values, space=pltpu.VMEM):
    return [pltpu.with_memory_space_constraint(item, space) for item in values]


def swap_pairs(count, first):
    pairs = []
    for low in range(first, count, 2):
        high = (low + 1) % count
        pairs += [(low, high), (high, low)]
    return pairs


EAST_HALO = 10


def own_columns(refs, rows):
    lane = lane_iota((rows[1], LANES))
    level, g = lane >> 4, lane & 15
    index = jnp.where(g < 6, jnp.maximum(g - 2, 0), jnp.minimum(g + (LANES - EAST_HALO), LANES - 1))
    both = jnp.zeros((rows[1], LANES), f32)
    for l, (first, second) in enumerate(refs):
        ends = jnp.where(lane < LANES // 2, first[pl.ds(*rows), :], second[pl.ds(*rows), :])
        moved = jnp.take_along_axis(ends, index, axis=1, mode="promise_in_bounds")
        both = moved if len(refs) == 1 else jnp.where(level == l, moved, both)
    return jnp.where((g >= 2) & (g < EAST_HALO), both, 0.0)


def join_strip(own, from_west, from_east, f):
    g = lane_iota(own.shape) & 15
    west = pltpu.roll(from_west, (-2 * f) % LANES, 1)
    east = pltpu.roll(from_east, (EAST_HALO - 2 * f) % LANES, 1)
    value = jnp.where(g < 2, west, own)
    return jnp.where((g >= EAST_HALO) & (g < EAST_HALO + 2), east, value)


def x_halos(first, second):
    gx = lax.axis_index("gx")
    even = gx % 2 == 0
    from_west = jnp.where(gx == 0, 0.0, jnp.where(even, second, first))
    from_east = jnp.where(gx == lax.axis_size("gx") - 1, 0.0, jnp.where(even, first, second))
    return from_west, from_east


def load_kernel(h_hbm, vel_hbm, bot_hbm, cor_hbm, red_hbm, h_ref, uv_ref, bc_ref, own_ref, a_ref, b_ref, red_ref,
                red, sem):
    levels, rows = h_hbm.shape[0], h_hbm.shape[1]
    body = pl.ds(PAD, rows)
    copies = []
    for t in range(2):
        cols = pl.ds(t * LANES, LANES)
        copies += [
            (h_hbm.at[:, :, cols], h_ref.at[:, t, body, :]),
            (vel_hbm.at[0, :, :, cols], uv_ref.at[0, :, t, body, :]),
            (vel_hbm.at[1, :, :, cols], uv_ref.at[1, :, t, body, :]),
            (bot_hbm.at[:, cols], bc_ref.at[0, t, body, :]),
            (cor_hbm.at[:, cols], bc_ref.at[1, t, body, :]),
        ]
    copies = [pltpu.make_async_copy(s, d, sem.at[i]) for i, (s, d) in enumerate(copies)]
    few = pltpu.make_async_copy(red_hbm, red, sem.at[10])
    for i in ORDER:
        copies[i].start()
        copies[5 + i].start()
    few.start()
    gx = lax.axis_index("gx")
    even = gx % 2 == 0
    step = CHUNK
    lane = lane_iota((step, LANES))
    wall = ((lane & 15) == EAST_HALO - 1) & (gx == lax.axis_size("gx") - 1)
    for f in ORDER:
        copies[f].wait()
        copies[5 + f].wait()
        if f < 3:
            ref = (h_ref, uv_ref.at[0], uv_ref.at[1])[f]
            refs = [(ref.at[l, 0], ref.at[l, 1]) for l in range(levels)]
        else:
            refs = [(bc_ref.at[f - 3, 0], bc_ref.at[f - 3, 1])]
        mine = ((lane & 15) >> 1) == f

        def chunk(k):
            start = k * step
            own = own_columns(refs, (start + PAD, step))
            if f == 1:
                own = jnp.where(wall, 0.0, own)
            own_ref[f, 0, pl.ds(start + PAD, step), :] = own
            west = pltpu.roll(own, (2 * f - 2) % LANES, 1)
            east = pltpu.roll(own, (2 * f - 8) % LANES, 1)
            for ref, value in ((a_ref, jnp.where(even, east, west)), (b_ref, jnp.where(even, west, east))):
                span = pl.ds(start, step)
                ref[span, :] = jnp.where(mine, value, 0.0 if f == ORDER[0] else ref[span, :])

        for k in range(rows // step):
            chunk(k)
    few.wait()
    for l in range(levels):
        red_ref[pl.ds(l, 1), :] = jnp.full((1, LANES), 2.0 * red[l], f32)


def rows_kernel(h_ref, bc_ref, uv_in, uv_ref, north_ref, south_ref, own, bc, late_bc):
    levels = h_ref.shape[0]
    rows = h_ref.shape[2] - 2 * PAD
    u_ref, v_ref = uv_ref.at[0], uv_ref.at[1]

    @pl.when(lax.axis_index("gx") == lax.axis_size("gx") - 1)
    def _():
        lane = lane_iota((rows, LANES))
        for l in range(levels):
            edge = u_ref[l, 1, pl.ds(PAD, rows), :]
            u_ref[l, 1, pl.ds(PAD, rows), :] = jnp.where(lane == LANES - 1, 0.0, edge)

    low, high = pl.ds(PAD, 2), pl.ds(PAD + rows - 2, 2)
    for src, dst in ((h_ref, own.at[0]), (u_ref, own.at[1]), (v_ref, own.at[2]), (bc_ref, bc)):
        for l in range(src.shape[0]):
            dst[l, :, pl.ds(PAD + 2, 2), :] = src[l, :, low, :]
            dst[l, :, pl.ds(PAD + 4, 2), :] = src[l, :, high, :]
    for f in range(2):
        late_bc[f, :, pl.ds(PAD + 1, 3), :] = bc_ref[f, :, pl.ds(PAD, 3), :]
        late_bc[f, :, pl.ds(PAD + 4, 3), :] = bc_ref[f, :, pl.ds(PAD + rows - 3, 3), :]
    for t in range(2):
        cols = pl.ds(t * LANES, LANES)
        for f, ref in enumerate((h_ref, u_ref, v_ref)):
            for l in range(levels):
                spot = pl.ds(2 * (f * levels + l), 2)
                north_ref[spot, cols] = ref[l, t, pl.ds(PAD + rows - 2, 2), :]
                south_ref[spot, cols] = ref[l, t, pl.ds(PAD, 2), :]
        for f in range(2):
            spot = pl.ds(2 * (3 * levels + f), 2)
            north_ref[spot, cols] = bc_ref[f, t, pl.ds(PAD + rows - 2, 2), :]
            south_ref[spot, cols] = bc_ref[f, t, pl.ds(PAD, 2), :]


def corner_kernel(north_in, south_in, own_ref, ra, rb, after, north_ref, south_ref):
    rows = ra.shape[0]
    north_ref[0:MAIN, :] = north_in[0:MAIN, :]
    south_ref[0:MAIN, :] = south_in[0:MAIN, :]

    def tail(start, f):
        span = pl.ds(start, 8)
        r1, r2 = ra[span, :], rb[span, :]
        own = own_ref[f, 0, pl.ds(PAD + start, 8), :]
        return join_strip(own, *x_halos(r1, r2), f)

    for f in range(5):
        up, down = tail(rows - 8, f), tail(0, f)
        for r in range(2):
            cols = pl.ds(LANES * r, LANES)
            north_ref[pl.ds(STRIP_ROWS[f][0], 1), cols] = up[6 + r : 7 + r, :]
            south_ref[pl.ds(STRIP_ROWS[f][1], 1), cols] = down[r : r + 1, :]


def evaluate(fields, temps, height, spin, east, west, reduced, rows, step, update):
    h_ref, u_ref, v_ref = fields
    s_ref, fx_ref, fy_ref, b_ref, z_ref, vq_ref = temps

    def span(k, shift=0):
        return pl.ds(PAD + k * step + shift, step)

    def cells(k):
        h, hn = h_ref[:, span(k), :], h_ref[:, span(k, 1), :]
        u, un = u_ref[:, span(k), :], u_ref[:, span(k, 1), :]
        v, vs = v_ref[:, span(k), :], v_ref[:, span(k, -1), :]
        pair = h + east(h)
        square = u * u
        kinetic = 0.5 * (square + west(square) + v * v + vs * vs)
        s_ref[:, span(k), :] = pair
        fx_ref[:, span(k), :] = pair * u
        fy_ref[:, span(k), :] = (h + hn) * v
        b_ref[:, span(k), :] = kinetic + (height(k) + reduced * h)
        z_ref[:, span(k), :] = (east(v) - v) - (un - u) + spin(k)

    def finish(k):
        pair, pair_n = s_ref[:, span(k), :], s_ref[:, span(k, 1), :]
        fx, fxn = fx_ref[:, span(k), :], fx_ref[:, span(k, 1), :]
        fy, fys = fy_ref[:, span(k), :], fy_ref[:, span(k, -1), :]
        b, bn = b_ref[:, span(k), :], b_ref[:, span(k, 1), :]
        q = z_ref[:, span(k), :] / (pair + pair_n)
        uq = q * (fx + fxn)
        vq = q * (fy + east(fy))
        vq_ref[:, span(k), :] = vq
        dh = (fx - west(fx)) + (fy - fys)
        dv = (west(uq) + uq) + (bn - b)
        du = (vq_ref[:, span(k, -1), :] + vq) - (east(b) - b)
        update(k, dh, du, dv)

    count = rows // step
    cells(0)
    for k in range(count):
        if k + 1 < count:
            cells(k + 1)
        finish(k)


def span_of(k, step):
    return pl.ds(PAD + k * step, step)


def level_sum(values):
    for shift in (16, 32, 64):
        values = values + pltpu.roll(values, shift, values.ndim - 1)
    return values


def base(h_at, bc, height, rows, step):
    for k in range(rows // step):
        total = bc[0, :, span_of(k, step), :]
        for l in range(h_at.shape[0]):
            total = total + h_at[l, :, span_of(k, step), :]
        height[:, span_of(k, step), :] = total


def main_stage(now, temps, height, bc, reduced, rows, step, unroll, update, after=None, low=0, high=None):
    lane = lane_iota((1, step, LANES))

    def east(x):
        moved = pltpu.roll(x, LANES - 1, 2)
        return jnp.concatenate([jnp.where(lane == LANES - 1, moved[1:2], moved[0:1]), moved[1:2]], axis=0)

    def west(x):
        moved = pltpu.roll(x, 1, 2)
        return jnp.concatenate([moved[0:1], jnp.where(lane == 0, moved[0:1], moved[1:2])], axis=0)

    def one(l, slot):
        evaluate(
            [ref.at[l] for ref in now],
            [temps.at[slot, i] for i in range(6)],
            lambda k: height[:, span_of(k, step), :],
            lambda k: bc[1, :, span_of(k, step), :],
            east, west, reduced[pl.ds(l, 1), :][None], rows, step,
            lambda k, dh, du, dv: update(l, k, (dh, du, dv)),
        )
        if after is not None:
            after(l)

    def single(l, carry):
        one(l, 0)
        return carry

    high = now[0].shape[0] if high is None else high
    if unroll == 1:
        lax.fori_loop(low, high, single, 0)
    else:
        for l in range(unroll):
            one(l, l)


def strip_masks(reduced, gx, size_x, step):
    g = lane_iota((1, step, LANES)) & 15
    west_out = (g < 2) & (gx == 0)
    out = west_out | ((g >= EAST_HALO) & (gx == size_x - 1))
    out_u = west_out | ((g >= EAST_HALO - 1) & (gx == size_x - 1))
    small = lane_iota((1, 1, LANES))
    red_lane = jnp.zeros((1, 1, LANES), f32)
    for l in range(8):
        red_lane = jnp.where((small >> 4) == l, reduced[l : l + 1, :][None], red_lane)
    return (out, out_u, out), red_lane


def strip_stage(now, strips, temps, red_lane, rows, step, update):
    evaluate(
        [now.at[i] for i in range(3)],
        [temps.at[i] for i in range(6)],
        lambda k: strips[3, :, span_of(k, step), :] + level_sum(now[0, :, span_of(k, step), :]),
        lambda k: strips[4, :, span_of(k, step), :],
        lambda x: pltpu.roll(x, LANES - 1, 2),
        lambda x: pltpu.roll(x, 1, 2),
        red_lane, rows, step, update,
    )


def strip_last(acc, out_u, step):
    g = lane_iota((1, step, LANES)) & 15

    def update(k, *rates):
        for i, rate in enumerate(rates):
            value = acc[i, :, span_of(k, step), :] + RATE[i] * half_step * rate
            value = jnp.where(out_u, 0.0, value) if i == 1 else value
            acc[i, :, span_of(k, step), :] = jnp.where(g < 2, pltpu.roll(value, LANES - 8, 2), value)

    return update


def strip_stages(strips, mid, acc, temps, reduced, gx, size_x, rows, step):
    masks, red_lane = strip_masks(reduced, gx, size_x, step)

    def first(k, *rates):
        for i, rate in enumerate(rates):
            start = strips[i, :, span_of(k, step), :]
            mid[i, :, span_of(k, step), :] = jnp.where(masks[i], 0.0, start + RATE[i] * time_step * rate)
            acc[i, :, span_of(k, step), :] = start + RATE[i] * half_step * rate

    strip_stage(strips, strips, temps, red_lane, rows, step, first)
    strip_stage(mid, strips, temps, red_lane, rows, step, strip_last(acc, masks[1], step))


def first_update(fields, mid, acc, late_mid, late_acc, step, last):
    def update(l, k, rates):
        for i, rate in enumerate(rates):
            start = fields[i][l, :, span_of(k, step), :]
            middle, total = start + RATE[i] * time_step * rate, start + RATE[i] * half_step * rate
            mid[i, l, :, span_of(k, step), :] = middle
            acc[i, l, :, pl.ds(k * step, step), :] = total
            if k == 0:
                late_mid[i, l, :, pl.ds(PAD + 2, 2), :] = middle[:, 1:3, :]
                late_acc[i, l, :, pl.ds(2, 1), :] = total[:, 1:2, :]
            if k == last:
                late_mid[i, l, :, pl.ds(PAD + 4, 2), :] = middle[:, step - 3 : step - 1, :]
                late_acc[i, l, :, pl.ds(5, 1), :] = total[:, step - 2 : step - 1, :]

    return update


def second_update(acc, strip, step, emit):
    lane = lane_iota((step, LANES))

    def update(l, k, rates):
        for i, rate in enumerate(rates):
            value = acc[i, l, :, pl.ds(k * step, step), :] + RATE[i] * half_step * rate
            edge = pltpu.roll(strip[i, 0, span_of(k, step), :], LANES - 2 - 16 * l, 1)
            emit(i, l, k, jnp.where(lane < 2, edge, value[0]), jnp.where(lane >= LANES - 2, edge, value[1]))

    return update


def first_kernel(h_ref, uv_ref, bc_ref, reduced, mid, acc, late_mid, late_acc, height, temps):
    fields = (h_ref, uv_ref.at[0], uv_ref.at[1])
    rows = h_ref.shape[2] - 2 * PAD
    step = 8
    base(h_ref, bc_ref, height, rows, step)
    main_stage(fields, temps, height, bc_ref, reduced, rows, step, 1,
               first_update(fields, mid, acc, late_mid, late_acc, step, rows // step - 1))


def prepare(own_ref, ra, rb, mid, bc_ref, reduced, strip_ref, strip_acc, height, strip_mid, strip_temps):
    gx, size_x = lax.axis_index("gx"), lax.axis_size("gx")
    rows = ra.shape[0]
    from_west, from_east = x_halos(ra[...], rb[...])
    for f in range(5):
        strip_ref[f, 0, pl.ds(PAD, rows), :] = join_strip(own_ref[f, 0, pl.ds(PAD, rows), :], from_west, from_east, f)
    strip_stages(strip_ref, strip_mid, strip_acc, strip_temps, reduced, gx, size_x, rows, 16)
    base(mid.at[0], bc_ref, height, rows, 8)


def second_levels(low, high, mid, acc, bc_ref, reduced, h_out, vel_out, edge_ref, strip_acc, height, result, sem, temps):
    rows = acc.shape[3]
    step = 8
    last = rows // step - 1
    body = pl.ds(step, rows - 2 * step)

    def emit(i, l, k, *tiles):
        for t, value in enumerate(tiles):
            if k == 0 or k == last:
                edge_ref[i, l, pl.ds(0 if k == 0 else step, step), pl.ds(t * LANES, LANES)] = value
            else:
                result[i, l, pl.ds(k * step, step), pl.ds(t * LANES, LANES)] = value

    def copies(l):
        targets = (h_out.at[l], vel_out.at[0, l], vel_out.at[1, l])
        return [
            pltpu.make_async_copy(result.at[i, l, body, :], target.at[body, :], sem.at[l, i])
            for i, target in enumerate(targets)
        ]

    main_stage([mid.at[i] for i in range(3)], temps, height, bc_ref, reduced, rows, step, 1,
               second_update(acc, strip_acc, step, emit), lambda l: [copy.start() for copy in copies(l)], low, high)

    def finish(l, carry):
        for copy in copies(l):
            copy.wait()
        return carry

    lax.fori_loop(low, high, finish, 0)


def store(result, h_out, vel_out, sem, spans):
    copies = []
    for src, dst in spans:
        copies += [
            (result.at[0, :, src, :], h_out.at[:, dst, :]),
            (result.at[1, :, src, :], vel_out.at[0, :, dst, :]),
            (result.at[2, :, src, :], vel_out.at[1, :, dst, :]),
        ]
    copies = [pltpu.make_async_copy(s, d, sem.at[i]) for i, (s, d) in enumerate(copies)]
    for copy in copies:
        copy.start()
    for copy in copies:
        copy.wait()


def early_count(levels):
    return jnp.clip(EARLY[0] - lax.axis_index("gy") * EARLY[1] // 2, 0, levels)


def early_kernel(own_ref, ra, rb, mid, acc, bc_ref, reduced, y_in, h_out, vel_out, edge_ref, strip_ref, strip_acc, height,
                 strip_mid, y_out, result, sem, temps, strip_temps):
    count = early_count(mid.shape[1])

    @pl.when(count > 0)
    def _():
        prepare(own_ref, ra, rb, mid, bc_ref, reduced, strip_ref, strip_acc, height, strip_mid, strip_temps)
        second_levels(0, count, mid, acc, bc_ref, reduced, h_out, vel_out, edge_ref, strip_acc, height, result, sem, temps)


def late_kernel(own_ref, ra, rb, mid, acc, bc_ref, reduced, h_in, vel_in, edge_in, strip_in, strip_acc_in, height_in,
                strip_mid_in, h_out, vel_out, edge_ref, strip_ref, strip_acc, height, strip_mid, result, sem, temps, strip_temps):
    levels = mid.shape[1]
    count = early_count(levels)

    @pl.when(count == 0)
    def _():
        prepare(own_ref, ra, rb, mid, bc_ref, reduced, strip_ref, strip_acc, height, strip_mid, strip_temps)

    @pl.when(count < levels)
    def _():
        second_levels(count, levels, mid, acc, bc_ref, reduced, h_out, vel_out, edge_ref, strip_acc, height, result, sem, temps)


def outer_kernel(strip_ref, strip_mid_ref, m0, m1, reduced, own_in, bc_in, late_bc_in, mid_in, acc_in, edge_in, h_in, vel_in,
                 h_out, vel_out, own, bc, late_bc, mid, acc, result, strips, late_strips, sem, strip_mid, strip_acc, height,
                 temps, strip_temps):
    gx, size_x = lax.axis_index("gx"), lax.axis_size("gx")
    levels = own.shape[1]
    rows = h_out.shape[1]
    south, north = m0[...], m1[...]

    for t in range(2):
        cols = slice(t * LANES, (t + 1) * LANES)

        def place(dst, index, spot):
            dst[(*index, t, pl.ds(PAD, 2), slice(None))] = south[spot : spot + 2, cols]
            dst[(*index, t, pl.ds(PAD + 6, 2), slice(None))] = north[spot : spot + 2, cols]

        for f in range(3):
            for l in range(levels):
                place(own, (f, l), 2 * (f * levels + l))
        for f in range(2):
            spot = 2 * (3 * levels + f)
            place(bc, (f,), spot)
            late_bc[f, t, pl.ds(PAD, 1), :] = south[spot + 1 : spot + 2, cols]
            late_bc[f, t, pl.ds(PAD + 7, 1), :] = north[spot : spot + 1, cols]
    for f in range(5):
        before = south[STRIP_ROWS[f][0] : STRIP_ROWS[f][0] + 1, :]
        after = north[STRIP_ROWS[f][1] : STRIP_ROWS[f][1] + 1, :]
        strips[f, 0, pl.ds(PAD, 1), :] = before[:, :LANES]
        strips[f, 0, pl.ds(PAD + 1, 1), :] = before[:, LANES:]
        strips[f, 0, pl.ds(PAD + 2, 2), :] = strip_ref[f, 0, pl.ds(PAD, 2), :]
        strips[f, 0, pl.ds(PAD + 4, 2), :] = strip_ref[f, 0, pl.ds(PAD + rows - 2, 2), :]
        strips[f, 0, pl.ds(PAD + 6, 1), :] = after[:, :LANES]
        strips[f, 0, pl.ds(PAD + 7, 1), :] = after[:, LANES:]
        if f >= 3:
            late_strips[f, 0, pl.ds(PAD, 1), :] = before[:, LANES:]
            late_strips[f, 0, pl.ds(PAD + 1, 3), :] = strip_ref[f, 0, pl.ds(PAD, 3), :]
            late_strips[f, 0, pl.ds(PAD + 4, 3), :] = strip_ref[f, 0, pl.ds(PAD + rows - 3, 3), :]
            late_strips[f, 0, pl.ds(PAD + 7, 1), :] = after[:, :LANES]
    for i in range(3):
        for src, dst, kept in ((1, 2, 1), (rows - 3, 4, rows - 2)):
            strip_mid[i, 0, pl.ds(PAD + dst, 2), :] = strip_mid_ref[i, 0, pl.ds(PAD + src, 2), :]
            start, middle = strip_ref[i, 0, pl.ds(PAD + kept, 1), :], strip_mid_ref[i, 0, pl.ds(PAD + kept, 1), :]
            strip_acc[i, 0, pl.ds(PAD + (2 if kept == 1 else 5), 1), :] = 0.5 * (start + middle)

    masks, red_lane = strip_masks(reduced, gx, size_x, 8)

    def strip_first(k, *rates):
        for i, rate in enumerate(rates):
            start = strips[i, :, span_of(0, 8), :]
            middle = jnp.where(masks[i], 0.0, start + RATE[i] * time_step * rate)
            total = start + RATE[i] * half_step * rate
            strip_mid[i, :, pl.ds(PAD, 2), :] = middle[:, 1:3, :]
            strip_mid[i, :, pl.ds(PAD + 6, 2), :] = middle[:, 5:7, :]
            strip_acc[i, :, pl.ds(PAD + 1, 1), :] = total[:, 2:3, :]
            strip_acc[i, :, pl.ds(PAD + 6, 1), :] = total[:, 5:6, :]

    strip_stage(strips, strips, strip_temps, red_lane, 8, 8, strip_first)
    strip_stage(strip_mid, late_strips, strip_temps, red_lane, 8, 8, strip_last(strip_acc, masks[1], 8))

    fields = [own.at[i] for i in range(3)]
    base(fields[0], bc, height, 8, 8)

    def first(l, k, rates):
        for i, rate in enumerate(rates):
            start = fields[i][l, :, span_of(0, 8), :]
            middle, total = start + RATE[i] * time_step * rate, start + RATE[i] * half_step * rate
            mid[i, l, :, pl.ds(PAD, 2), :] = middle[:, 1:3, :]
            mid[i, l, :, pl.ds(PAD + 6, 2), :] = middle[:, 5:7, :]
            acc[i, l, :, pl.ds(1, 1), :] = total[:, 2:3, :]
            acc[i, l, :, pl.ds(6, 1), :] = total[:, 5:6, :]

    main_stage(fields, temps, height, bc, reduced, 8, 8, levels, first)
    base(mid.at[0], late_bc, height, 8, 8)

    def emit(i, l, k, *tiles):
        for t, value in enumerate(tiles):
            cols = pl.ds(t * LANES, LANES)
            result[i, l, pl.ds(0, 2), cols] = value[1:3, :]
            result[i, l, pl.ds(14, 2), cols] = value[5:7, :]

    main_stage([mid.at[i] for i in range(3)], temps, height, late_bc, reduced, 8, 8, levels,
               second_update(acc, strip_acc, 8, emit))
    store(result, h_out, vel_out, sem, ((pl.ds(0, 8), pl.ds(0, 8)), (pl.ds(8, 8), pl.ds(rows - 8, 8))))


def body(thickness, velocity, bottom, coriolis, reduced):
    levels, rows, columns = thickness.shape
    total = rows + 2 * PAD
    field = VM((levels, 2, total, LANES), f32)
    strip = VM((5, 1, total, LANES), f32)
    message_x, message_y = VM((rows, LANES), f32), VM((56, 2 * LANES), f32)
    h_shape = jax.ShapeDtypeStruct(thickness.shape, f32)
    vel_shape = jax.ShapeDtypeStruct(velocity.shape, f32)
    edge_shape = VM((3, levels, 16, 2 * LANES), f32)

    def call(kernel, name, out_shape, in_specs, args, out_specs=None, scratch=(), limit=SMALL, aliases={}):
        return pl.pallas_call(
            kernel,
            out_shape=out_shape,
            in_specs=in_specs,
            out_specs=out_specs or [VSPEC] * len(out_shape),
            scratch_shapes=list(scratch),
            input_output_aliases=aliases,
            compiler_params=pltpu.CompilerParams(vmem_limit_bytes=limit),
            name=name,
        )(*args)

    size_x, size_y = lax.axis_size("gx"), lax.axis_size("gy")

    args = pin((thickness, velocity, bottom, coriolis, reduced), pltpu.HBM)
    uv_shape = VM((2, levels, 2, total, LANES), f32)
    h, uv, bc, own, sa, sb, red = pin(call(
        load_kernel, "load",
        [field, uv_shape, VM((2, 2, total, LANES), f32), strip, message_x, message_x, VM((levels, LANES), f32)],
        [ASPEC] * 5, args,
        scratch=[
            pltpu.SMEM((levels,), f32),
            pltpu.SemaphoreType.DMA((11,)),
        ],
    ))
    ra, rb = pin([lax.ppermute(item, "gx", swap_pairs(size_x, i)) for i, item in enumerate((sa, sb))])
    edge_fields, edge_fixed = VM((3, levels, 2, 24, LANES), f32), VM((2, 2, 24, LANES), f32)
    edge_sums = VM((3, levels, 2, 8, LANES), f32)
    uv, north, south, own_edge, bc_edge, late_bc = pin(call(
        rows_kernel, "edges", [uv_shape] + [message_y] * 2 + [edge_fields, edge_fixed, edge_fixed], [VSPEC] * 3, (h, bc, uv),
        aliases={2: 0},
    ))
    temps = VM((1, 6, 2, total, LANES), f32)
    strip_temps = VM((6, 1, total, LANES), f32)
    strip_part, height = VM((3, 1, total, LANES), f32), VM((2, total, LANES), f32)
    mid, acc, late_mid, late_acc = pin(call(
        first_kernel, "first",
        [VM((3, levels, 2, total, LANES), f32), VM((3, levels, 2, rows, LANES), f32), edge_fields, edge_sums],
        [VSPEC] * 4, (h, uv, bc, red), scratch=[height, temps],
    ))
    y0, y1 = pin(call(
        corner_kernel, "corners", [message_y] * 2, [VSPEC] * 6, (north, south, own, ra, rb, mid),
    ))
    (m0,) = pin([lax.ppermute(y0, "gy", [(i, (i + 1) % size_y) for i in range(size_y)])])
    work = [VM((3, levels, rows, 2 * LANES), f32), pltpu.SemaphoreType.DMA((levels, 3)), temps, strip_temps]
    outs = [h_shape, vel_shape, edge_shape, strip, strip_part, height, strip_part]
    specs = [ASPEC, ASPEC] + [VSPEC] * 5
    h_new, vel_new, *kept, y1 = call(
        early_kernel, "early", outs + [message_y], [VSPEC] * 8,
        (own, ra, rb, mid, acc, bc, red, y1), specs + [VSPEC], work, LARGE, {7: 7},
    )
    *kept, y1 = pin([*kept, y1])
    (m1,) = pin([lax.ppermute(y1, "gy", [(i, (i - 1) % size_y) for i in range(size_y)])])
    h_new, vel_new, edge, strips, _, _, strip_mid = call(
        late_kernel, "late", outs, [VSPEC] * 7 + [ASPEC, ASPEC] + [VSPEC] * 5,
        (own, ra, rb, mid, acc, bc, red, h_new, vel_new, *kept), specs, work, LARGE,
        {7 + i: i for i in range(7)},
    )
    edge, strips, strip_mid = pin([edge, strips, strip_mid])
    part = VM((3, 1, 24, LANES), f32)
    strip_small = VM((5, 1, 24, LANES), f32)
    return tuple(call(
        outer_kernel, "outer",
        [h_shape, vel_shape, edge_fields, edge_fixed, edge_fixed, edge_fields, edge_sums, edge_shape],
        [VSPEC] * 11 + [ASPEC, ASPEC],
        (strips, strip_mid, m0, m1, red, own_edge, bc_edge, late_bc, late_mid, late_acc, edge, h_new, vel_new),
        [ASPEC, ASPEC] + [VSPEC] * 6,
        [
            strip_small,
            strip_small,
            pltpu.SemaphoreType.DMA((6,)),
            part,
            part,
            VM((2, 24, LANES), f32),
            VM((levels, 6, 2, 24, LANES), f32),
            VM((6, 1, 24, LANES), f32),
        ],
        LARGE, {11: 0, 12: 1, 5: 2, 6: 3, 7: 4, 8: 5, 9: 6, 10: 7},
    )[:2])


def solution(mesh):
    return jax.shard_map(
        body,
        mesh=mesh,
        in_specs=(
            P(None, "gy", "gx"),
            P(None, None, "gy", "gx"),
            P("gy", "gx"),
            P("gy", "gx"),
            P(),
        ),
        out_specs=(P(None, "gy", "gx"), P(None, None, "gy", "gx")),
        check_vma=False,
    )
```
